512 devices in a mesh: rep: 4 (over x), ep: 128 (over z, y, core).
Axes of the slice: x: 4, y: 8, z: 8, core: 2. Of those that a mesh axis runs over, the one named last changes fastest.
Arguments:
- tokens: bfloat16 [16384, 2048], P('ep', 'rep'), may hold values from -6 to 6
- out_grad: bfloat16 [16384, 2048], P('ep', 'rep'), may hold values from -6 to 6
- expert_ids: int32 [16384, 8], P('ep'), may hold values from 0 to 127, all different within a row; in each aligned block of 128 rows (0 to 127, 128 to 255, ...) at most 9 rows name the same one
- route_weight: bfloat16 [16384, 8], P('ep'), may hold values from 0.019897461 to 0.29882812
- w_gate: bfloat16 [128, 2048, 640], P('ep', 'rep'), may hold values from -0.125 to 0.125
- w_up: bfloat16 [128, 2048, 640], P('ep', 'rep'), may hold values from -0.125 to 0.125
- w_down: bfloat16 [128, 640, 2048], P('ep', None, 'rep'), may hold values from -0.25 to 0.25
Outputs:
- token_grad: bfloat16 [16384, 2048], P('ep', 'rep')
- grad_gate: bfloat16 [128, 2048, 640], P('ep', 'rep')
- grad_up: bfloat16 [128, 2048, 640], P('ep', 'rep')
- grad_down: bfloat16 [128, 640, 2048], P('ep', None, 'rep')
The draws below stay inside these ranges and needn't reach their ends.
Inputs may be any that keep to these rules, and one draw needn't show every extreme that they name: `expert_ids`: each token picks 8 different experts. Among the 128 tokens of one index of ep no expert is picked by more than 9 tokens, and in every draw some expert is picked by exactly 9 tokens of some such index.
All inputs are finite; a program needn't handle non-finite values.
Results may differ from the reference program's by a relative error of at most 0.024.
Values may be sent and summed in bfloat16 or wider, within the bound.
No kernel may reach another device: no remote copies, remote signals or barrier semaphores. Data moves between devices by JAX's collectives and lax.ppermute only.
A program may use at most 64 MiB of HBM per device.

```python
import math
import jax
import jax.numpy as jnp
import numpy as np
from jax import lax

D = 2048
E = 128
TOP = 8
FFW = 640
TOK_DEV = 128
TOKENS = 16384
CAP = 9
N_REP = 4
N_EP = 128


def levels(own_key, dims, shards, smallest, largest):
    level, own = 1.0, jax.random.fold_in(own_key, 6)
    for dim, parts in shards:
        heights = jnp.exp(jax.random.uniform(jax.random.fold_in(own, dim), (parts,), jnp.float32, smallest / len(shards), largest / len(shards)))
        level = level * jnp.repeat(heights, dims[dim] // parts).reshape([-1 if axis == dim else 1 for axis in range(len(dims))])
    return level


def shared_out(own_key, own, number, rows, amount, top, most, lean):
    order = jax.random.permutation(own_key, amount)
    crowded, ordinary = shares(amount, rows * top, most, lean, True), shares(amount, rows * top, most, lean, False)
    places = jnp.arange(amount)

    def named(tallies, offset_by):
        used = int((tallies > 0).sum())
        fixed = max(1, used // 4)
        shifted = fixed + (places - fixed + offset_by * (used - fixed)) % max(1, amount - fixed)
        return jnp.zeros((amount,), jnp.int32).at[order[jnp.where(places < fixed, places, shifted)]].set(jnp.asarray(tallies, jnp.int32))

    tallies = jnp.where(number % 4 == 0, named(crowded, number // 4), named(ordinary, number - number // 4 - 1))
    mixed = jax.random.permutation(jax.random.fold_in(own, 3), amount)
    source_of, taker = mixed[0:amount // 2 * 2:2], mixed[1:amount // 2 * 2:2]
    margin = jnp.minimum(tallies[source_of] - 1, most - tallies[taker]) // 2
    margin = jnp.where((source_of == order[0]) | (taker == order[0]) | (tallies[taker] == 0), 0, jnp.maximum(margin, 0))
    shifted = jax.random.randint(jax.random.fold_in(own, 4), (amount // 2,), 0, 1 << 20) % (margin + 1)
    tallies = tallies.at[source_of].add(-shifted).at[taker].add(shifted)
    members = jnp.searchsorted(jnp.cumsum(tallies), jnp.arange(rows * top), side="right").astype(jnp.int32)
    grid = members.reshape(top, rows).T
    grid = grid[jax.random.permutation(jax.random.fold_in(own, 1), rows)]
    offset_by = jax.random.randint(jax.random.fold_in(own, 2), (rows, 1), 0, top)
    return jnp.take_along_axis(grid, (jnp.arange(top)[None, :] + offset_by) % top, axis=1)


def shares(amount, total, limit, slope, full):
    loads = [(1 << 20) // math.isqrt(standing ** slope) + 1 for standing in range(1, amount + 1)]
    largest = limit if full else min(limit, max(-(-total // amount), total * loads[0] // sum(loads)))
    least = 1 if total - largest >= amount - 1 else 0
    holding, spare = [largest] + [least] * (amount - 1), total - largest - least * (amount - 1)
    while spare > 0:
        candidates = [i for i in range(1, amount) if holding[i] < largest] or [i for i in range(1, amount) if holding[i] < limit]
        whole, left = sum([loads[i] for i in candidates]), spare
        for i in candidates:
            extra = min(limit - holding[i], max(1, left * loads[i] // whole), spare)
            holding[i] = holding[i] + extra
            spare = spare - extra
    return np.array(holding)


def normal_values(rng, shape, scale, most, cuts=(), held_as=jnp.bfloat16):
    entries = scale * jax.random.normal(rng, shape, jnp.float32)
    if cuts:
        entries = entries * levels(rng, shape, cuts, -0.22, 0.18)
    return jnp.clip(entries, -most, most).astype(held_as)


def setup_inputs(seed: int = 0) -> dict:
    keys = jax.random.split(jax.random.key(seed), 8)
    tokens = normal_values(keys[0], (TOKENS, D), 1.0, 6.0, ((0, 128), (1, 4)))
    out_grad = normal_values(keys[1], (TOKENS, D), 1.0, 6.0, ((0, 128), (1, 4)))
    expert_ids_keys = jax.random.split(jax.random.fold_in(keys[2], 1), TOKENS // TOK_DEV)
    expert_ids_turns = jax.random.permutation(jax.random.fold_in(keys[2], 3), TOKENS // TOK_DEV)
    expert_ids = jax.vmap(lambda own, number: shared_out(jax.random.fold_in(keys[2], 2), own, number, TOK_DEV, E, TOP, CAP, 1))(expert_ids_keys, expert_ids_turns).reshape((TOKENS, TOP))
    route_weight = jnp.clip(0.019897461 + 0.27893066 * jax.random.uniform(keys[3], (TOKENS, TOP), jnp.float32) ** levels(keys[3], (TOKENS, TOP), ((0, 128),), -0.2, 0.2), 0.019897461, 0.29882812).astype(jnp.bfloat16)
    w_gate = normal_values(keys[4], (E, D, FFW), D ** -0.5, 0.125, ((0, 128), (1, 4)))
    w_up = normal_values(keys[5], (E, D, FFW), D ** -0.5, 0.125, ((0, 128), (1, 4)))
    w_down = normal_values(keys[6], (E, FFW, D), FFW ** -0.5, 0.25, ((0, 128), (2, 4)))
    return dict(tokens=tokens, out_grad=out_grad, expert_ids=expert_ids, route_weight=route_weight, w_gate=w_gate, w_up=w_up, w_down=w_down)


def hidden_terms(pre_gate, pre_up, pre_back, weight):
    sigmoid_gate = jax.nn.sigmoid(pre_gate)
    silu_gate = pre_gate * sigmoid_gate
    d_hidden = weight[..., None] * pre_back
    hidden = (silu_gate * pre_up).astype(jnp.bfloat16)
    gate_delta = (d_hidden * pre_up * sigmoid_gate * (1.0 + pre_gate * (1.0 - sigmoid_gate))).astype(jnp.bfloat16)
    up_delta = (d_hidden * silu_gate).astype(jnp.bfloat16)
    return hidden, gate_delta, up_delta


def quarter_sum(left_side, right_side, pattern):
    partials = jnp.einsum(pattern, left_side.astype(jnp.float32), right_side.astype(jnp.float32))
    rounded = lax.optimization_barrier(partials.astype(jnp.bfloat16))
    return jnp.sum(rounded.astype(jnp.float32), axis=0)


def reference(tokens, out_grad, expert_ids, route_weight, w_gate, w_up, w_down):
    token_count = tokens.shape[0]
    width = tokens.shape[1]
    quarter = width // N_REP
    column_rows = token_count // N_EP
    slot_rows = N_EP * CAP
    expert_range = jnp.arange(E, dtype=jnp.int32)
    matches = expert_ids[:, :, None] == expert_range[None, None, :]
    picked = jnp.sum(matches.astype(jnp.int32), axis=1).astype(jnp.int32).reshape(N_EP, column_rows, E)
    before = (jnp.cumsum(picked, axis=1).astype(jnp.int32) - picked).reshape(token_count, E)
    position = jnp.sum(jnp.where(matches, before[:, None, :], 0), axis=2).astype(jnp.int32)
    column = (jnp.arange(token_count, dtype=jnp.int32) // column_rows).astype(jnp.int32)[:, None]
    row_slot = (column * CAP + position).astype(jnp.int32)
    token_index = jnp.broadcast_to(jnp.arange(token_count, dtype=jnp.int32)[:, None], expert_ids.shape)
    pick_index = jnp.broadcast_to(jnp.arange(TOP, dtype=jnp.int32)[None, :], expert_ids.shape)
    slot_table = jnp.full((E, slot_rows), token_count, jnp.int32).at[expert_ids, row_slot].set(token_index)
    pick_table = jnp.zeros((E, slot_rows), jnp.int32).at[expert_ids, row_slot].set(pick_index)
    padded_tokens = jnp.concatenate([tokens, jnp.zeros((1, width), tokens.dtype)], axis=0)
    padded_grads = jnp.concatenate([out_grad, jnp.zeros((1, width), out_grad.dtype)], axis=0)
    padded_weight = jnp.concatenate([route_weight, jnp.zeros((1, TOP), route_weight.dtype)], axis=0)

    def per_expert(running, inputs):
        slot_tokens, slot_picks, gate_e, up_e, down_e = inputs
        rows_in = padded_tokens[slot_tokens]
        rows_grad = padded_grads[slot_tokens]
        weight = padded_weight[slot_tokens, slot_picks].astype(jnp.float32)
        split_in = rows_in.reshape(slot_rows, N_REP, quarter)
        split_grad = rows_grad.reshape(slot_rows, N_REP, quarter)
        pre_gate = quarter_sum(split_in, gate_e.reshape(N_REP, quarter, FFW), 'rqd,qdf->qrf')
        pre_up = quarter_sum(split_in, up_e.reshape(N_REP, quarter, FFW), 'rqd,qdf->qrf')
        pre_back = quarter_sum(split_grad, down_e.reshape(FFW, N_REP, quarter), 'rqd,fqd->qrf')
        hidden, gate_delta, up_delta = hidden_terms(pre_gate, pre_up, pre_back, weight)
        scaled_grad = (weight[:, None] * rows_grad.astype(jnp.float32)).astype(jnp.bfloat16)
        back_rows = jnp.dot(gate_delta, gate_e.T, preferred_element_type=jnp.float32)
        back_rows = back_rows + jnp.dot(up_delta, up_e.T, preferred_element_type=jnp.float32)
        back_rows = back_rows.astype(jnp.bfloat16)
        running = running.at[slot_tokens].add(back_rows.astype(jnp.float32))
        gate_grad = jnp.dot(rows_in.T, gate_delta, preferred_element_type=jnp.float32).astype(jnp.bfloat16)
        up_grad = jnp.dot(rows_in.T, up_delta, preferred_element_type=jnp.float32).astype(jnp.bfloat16)
        down_grad = jnp.dot(hidden.T, scaled_grad, preferred_element_type=jnp.float32).astype(jnp.bfloat16)
        return running, (gate_grad, up_grad, down_grad)

    start = jnp.zeros((token_count + 1, width), jnp.float32)
    token_sum, expert_grads = lax.scan(per_expert, start, (slot_table, pick_table, w_gate, w_up, w_down))
    token_grad = token_sum[:token_count].astype(jnp.bfloat16)
    return token_grad, expert_grads[0], expert_grads[1], expert_grads[2]
```

```python
import jax
import jax.numpy as jnp
from jax import lax
from jax.experimental import pallas as pl
from jax.experimental.pallas import tpu as pltpu
from jax.sharding import PartitionSpec as P

MAIN = 8
LANES = 128
BF = jnp.bfloat16
F32 = jnp.float32
CONTRACT_LAST = (((1,), (1,)), ((), ()))
CONTRACT_FIRST = (((0,), (0,)), ((), ()))


def dot(a, b, dims=(((1,), (0,)), ((), ()))):
    return lax.dot_general(a, b, dims, preferred_element_type=F32)


def kernel_call(body, out_shape, args, flops, scratch=()):
    moved = sum(a.size * a.dtype.itemsize for a in args)
    outs = out_shape if isinstance(out_shape, tuple) else (out_shape,)
    moved += sum(o.size * o.dtype.itemsize for o in outs)
    return pl.pallas_call(
        body,
        out_shape=out_shape,
        in_specs=[pl.BlockSpec(memory_space=pltpu.VMEM)] * len(args),
        out_specs=jax.tree.map(lambda _: pl.BlockSpec(memory_space=pltpu.VMEM), out_shape),
        scratch_shapes=list(scratch),
        compiler_params=pltpu.CompilerParams(vmem_limit_bytes=48 << 20),
        cost_estimate=pl.CostEstimate(flops=flops, bytes_accessed=moved, transcendentals=0),
    )(*args)


def routing(ids_ref, experts):
    top, count = ids_ref.shape
    expert = lax.broadcasted_iota(jnp.int32, (experts, count), 0)
    matches = [expert == ids_ref[k : k + 1, :] for k in range(top)]
    picked = sum(m.astype(F32) for m in matches)
    earlier = lax.broadcasted_iota(jnp.int32, (count, count), 0) < lax.broadcasted_iota(
        jnp.int32, (count, count), 1
    )
    before = dot(picked.astype(BF), earlier.astype(F32).astype(BF))
    return jnp.where(picked > 0.0, before, -1.0), matches


def spread(per_expert):
    experts, count = per_expert.shape
    wide = jnp.broadcast_to(per_expert[:, None, :], (experts, MAIN, count))
    return wide.reshape(experts * MAIN, count)


def main_slots(slot):
    experts, count = slot.shape
    number = lax.broadcasted_iota(jnp.int32, (experts * MAIN, count), 0) % MAIN
    return spread(slot) == number.astype(F32)


def dispatch_kernel(ids_ref, weight_ref, tokens_ref, grads_ref, first_ref, second_ref, packed):
    experts = first_ref.shape[0] // MAIN
    quarter = tokens_ref.shape[1]
    slot, matches = routing(ids_ref, experts)
    weight = sum(
        jnp.where(m, weight_ref[k : k + 1, :], 0.0) for k, m in enumerate(matches)
    )
    here = main_slots(slot)
    first_ref[...] = dot(jnp.where(here, 1.0, 0.0).astype(BF), tokens_ref[...]).astype(BF)
    second_ref[:, :quarter] = dot(
        jnp.where(here, spread(weight), 0.0).astype(BF), grads_ref[...]
    ).astype(BF)
    last = slot == float(MAIN)
    extra_tokens = dot(jnp.where(last, 1.0, 0.0).astype(BF), tokens_ref[...])
    extra_grads = dot(jnp.where(last, weight, 0.0).astype(BF), grads_ref[...])
    pieces = quarter // LANES
    for j in range(pieces):
        packed[:, j, :] = extra_tokens[:, j * LANES : (j + 1) * LANES]
        packed[:, pieces + j, :] = extra_grads[:, j * LANES : (j + 1) * LANES]
    second_ref[:, quarter:] = packed[...].reshape(experts * MAIN, LANES).astype(BF)


def token_products_kernel(rows_ref, gate_ref, up_ref, out_ref):
    ffw = gate_ref.shape[1]
    for r in range(4):
        n = rows_ref.shape[0] // 4
        rows = rows_ref[r * n : (r + 1) * n, :]
        out_ref[r * n : (r + 1) * n, :ffw] = dot(rows, gate_ref[...]).astype(BF)
        out_ref[r * n : (r + 1) * n, ffw:] = dot(rows, up_ref[...]).astype(BF)


def grad_products_kernel(
    rows_ref, gate_ref, up_ref, down_ref, out_ref, extra_tokens_ref, extra_grads_ref, packed
):
    quarter = gate_ref.shape[0]
    sources = rows_ref.shape[0] // MAIN
    pieces = quarter // LANES
    packed[...] = rows_ref[:, quarter:].astype(F32).reshape(sources, MAIN, LANES)
    for j in range(pieces):
        extra_tokens_ref[:, j * LANES : (j + 1) * LANES] = packed[:, j, :].astype(BF)
        extra_grads_ref[:, j * LANES : (j + 1) * LANES] = packed[:, pieces + j, :].astype(BF)
    extra = (
        dot(extra_tokens_ref[...], gate_ref[...]).astype(BF),
        dot(extra_tokens_ref[...], up_ref[...]).astype(BF),
        dot(extra_grads_ref[...], down_ref[...], CONTRACT_LAST).astype(BF),
    )
    n = rows_ref.shape[0] // 4
    m = sources // 4
    for r in range(4):
        at = r * (n + 3 * m)
        rows = rows_ref[r * n : (r + 1) * n, :quarter]
        out_ref[at : at + n, :] = dot(rows, down_ref[...], CONTRACT_LAST).astype(BF)
        for i in range(3):
            out_ref[at + n + i * m : at + n + (i + 1) * m, :] = extra[i][r * m : (r + 1) * m, :]


def hidden_kernel(tokens_side_ref, grads_side_ref, delta_ref, hidden_ref):
    n = tokens_side_ref.shape[0]
    ffw = grads_side_ref.shape[1]
    m = (grads_side_ref.shape[0] - n) // 3

    def terms(gate, up, back, at, size):
        gate, up, back = gate.astype(F32), up.astype(F32), back.astype(F32)
        sigmoid = 1.0 / (1.0 + jnp.exp(-gate))
        silu = gate * sigmoid
        hidden_ref[at : at + size, :] = (silu * up).astype(BF)
        delta_ref[at : at + size, :ffw] = (
            back * up * sigmoid * (1.0 + gate * (1.0 - sigmoid))
        ).astype(BF)
        delta_ref[at : at + size, ffw:] = (back * silu).astype(BF)

    terms(tokens_side_ref[:, :ffw], tokens_side_ref[:, ffw:], grads_side_ref[:n, :], 0, n)
    terms(
        grads_side_ref[n : n + m, :],
        grads_side_ref[n + m : n + 2 * m, :],
        grads_side_ref[n + 2 * m :, :],
        n,
        m,
    )


def back_kernel(delta_ref, gate_ref, up_ref, out_ref, packed):
    quarter, ffw = gate_ref.shape
    n = out_ref.shape[0] // 4
    m = n // MAIN
    for r in range(4):
        at = r * (n + m)
        rows = dot(delta_ref[at : at + n + m, :ffw], gate_ref[...], CONTRACT_LAST)
        rows = rows + dot(delta_ref[at : at + n + m, ffw:], up_ref[...], CONTRACT_LAST)
        out_ref[r * n : (r + 1) * n, :quarter] = rows[:n, :].astype(BF)
        for j in range(quarter // LANES):
            packed[r * m : (r + 1) * m, j, :] = rows[n:, j * LANES : (j + 1) * LANES]
    for j in range(quarter // LANES, MAIN):
        packed[:, j, :] = jnp.zeros((4 * m, LANES), F32)
    out_ref[:, quarter:] = packed[...].reshape(4 * n, LANES).astype(BF)


def token_weights_kernel(rows_ref, extra_ref, delta_ref, gate_ref, up_ref):
    ffw = gate_ref.shape[1]
    n = rows_ref.shape[0] // 4
    m = extra_ref.shape[0] // 4
    total = None
    for r in range(4):
        at = r * (n + m)
        part = dot(rows_ref[r * n : (r + 1) * n, :], delta_ref[at : at + n, :], CONTRACT_FIRST)
        part = part + dot(
            extra_ref[r * m : (r + 1) * m, :], delta_ref[at + n : at + n + m, :], CONTRACT_FIRST
        )
        total = part if total is None else total + part
    gate_ref[...] = total[:, :ffw].astype(BF)
    up_ref[...] = total[:, ffw:].astype(BF)


def down_weights_kernel(rows_ref, extra_ref, hidden_ref, down_ref):
    quarter = extra_ref.shape[1]
    n = rows_ref.shape[0] // 4
    m = extra_ref.shape[0] // 4
    total = None
    for r in range(4):
        at = r * (n + m)
        part = dot(
            hidden_ref[at : at + n, :], rows_ref[r * n : (r + 1) * n, :quarter], CONTRACT_FIRST
        )
        part = part + dot(
            hidden_ref[at + n : at + n + m, :], extra_ref[r * m : (r + 1) * m, :], CONTRACT_FIRST
        )
        total = part if total is None else total + part
    down_ref[...] = total.astype(BF)


def combine_kernel(ids_ref, rows_ref, out_ref, packed):
    experts = rows_ref.shape[0] // MAIN
    quarter = out_ref.shape[1]
    slot, _ = routing(ids_ref, experts)
    here = jnp.where(main_slots(slot), 1.0, 0.0).astype(BF)
    last = jnp.where(slot == float(MAIN), 1.0, 0.0).astype(BF)
    packed[...] = rows_ref[:, quarter:].astype(F32).reshape(experts, MAIN, LANES)
    total = dot(here, rows_ref[:, :quarter], CONTRACT_FIRST)
    for j in range(quarter // LANES):
        at = slice(j * LANES, (j + 1) * LANES)
        extra = dot(last, packed[:, j, :].astype(BF), CONTRACT_FIRST)
        out_ref[:, at] = (total[:, at] + extra).astype(BF)


def body(tokens, out_grad, expert_ids, route_weight, w_gate, w_up, w_down):
    experts = lax.axis_size("ep")
    count, quarter = tokens.shape
    w_gate, w_up, w_down = w_gate[0], w_up[0], w_down[0]
    ffw = w_gate.shape[1]
    main = experts * MAIN
    local = main // 4
    extra = experts // 4
    shape = jax.ShapeDtypeStruct
    packed = pltpu.VMEM((experts, MAIN, LANES), F32)

    def exchange(rows):
        blocks = rows.reshape(experts, MAIN, rows.shape[1])
        blocks = lax.all_to_all(blocks, "ep", split_axis=0, concat_axis=0, tiled=True)
        return blocks.reshape(rows.shape)

    ids = expert_ids.T
    first, second = kernel_call(
        dispatch_kernel,
        (shape((main, quarter), BF), shape((main, quarter + LANES), BF)),
        (ids, route_weight.T.astype(F32), tokens, out_grad),
        4 * main * count * quarter,
        (packed,),
    )
    token_rows = exchange(first)
    token_rows, second = lax.optimization_barrier((token_rows, second))
    grad_rows = exchange(second)
    products = kernel_call(
        token_products_kernel,
        shape((main, 2 * ffw), BF),
        (token_rows, w_gate, w_up),
        4 * main * quarter * ffw,
    )
    tokens_side = lax.psum_scatter(products, "rep", scatter_dimension=0, tiled=True)
    products, extra_tokens, extra_grads = kernel_call(
        grad_products_kernel,
        (
            shape((main + 3 * experts, ffw), BF),
            shape((experts, quarter), BF),
            shape((experts, quarter), BF),
        ),
        (grad_rows, w_gate, w_up, w_down),
        2 * (main + 3 * experts) * quarter * ffw,
        (packed,),
    )
    grads_side = lax.psum_scatter(products, "rep", scatter_dimension=0, tiled=True)
    delta, hidden = kernel_call(
        hidden_kernel,
        (shape((local + extra, 2 * ffw), BF), shape((local + extra, ffw), BF)),
        (tokens_side, grads_side),
        20 * (local + extra) * ffw,
    )
    delta = lax.all_gather(delta, "rep", axis=0, tiled=True)
    delta, hidden = lax.optimization_barrier((delta, hidden))
    hidden = lax.all_gather(hidden, "rep", axis=0, tiled=True)
    back = kernel_call(
        back_kernel,
        shape((main, quarter + LANES), BF),
        (delta, w_gate, w_up),
        4 * (main + experts) * quarter * ffw,
        (packed,),
    )
    returned = exchange(back)
    grad_gate, grad_up = kernel_call(
        token_weights_kernel,
        (shape((quarter, ffw), BF), shape((quarter, ffw), BF)),
        (token_rows, extra_tokens, delta),
        4 * (main + experts) * quarter * ffw,
    )
    grad_down = kernel_call(
        down_weights_kernel,
        shape((ffw, quarter), BF),
        (grad_rows, extra_grads, hidden),
        2 * (main + experts) * quarter * ffw,
    )
    token_grad = kernel_call(
        combine_kernel,
        shape((count, quarter), BF),
        (ids, returned),
        2 * main * count * quarter,
        (packed,),
    )
    return token_grad, grad_gate[None], grad_up[None], grad_down[None]


def solution(mesh):
    rows = P("ep", "rep")
    by_width = P("ep", "rep", None)
    last = P("ep", None, "rep")
    return jax.shard_map(
        body,
        mesh=mesh,
        in_specs=(rows, rows, P("ep", None), P("ep", None), by_width, by_width, last),
        out_specs=(rows, by_width, by_width, last),
        check_vma=False,
    )
```

```python
import jax
import jax.numpy as jnp
from jax import lax
from jax.experimental import pallas as pl
from jax.experimental.pallas import tpu as pltpu
from jax.sharding import PartitionSpec as P

MAIN = 8
LANES = 128
BF = jnp.bfloat16
F32 = jnp.float32
CONTRACT_LAST = (((1,), (1,)), ((), ()))
CONTRACT_FIRST = (((0,), (0,)), ((), ()))


def dot(a, b, dims=(((1,), (0,)), ((), ()))):
    return lax.dot_general(a, b, dims, preferred_element_type=F32)


def kernel_call(body, out_shape, args, flops, scratch=()):
    moved = sum(a.size * a.dtype.itemsize for a in args)
    outs = out_shape if isinstance(out_shape, tuple) else (out_shape,)
    moved += sum(o.size * o.dtype.itemsize for o in outs)
    return pl.pallas_call(
        body,
        out_shape=out_shape,
        in_specs=[pl.BlockSpec(memory_space=pltpu.VMEM)] * len(args),
        out_specs=jax.tree.map(lambda _: pl.BlockSpec(memory_space=pltpu.VMEM), out_shape),
        scratch_shapes=list(scratch),
        compiler_params=pltpu.CompilerParams(vmem_limit_bytes=48 << 20),
        cost_estimate=pl.CostEstimate(flops=flops, bytes_accessed=moved, transcendentals=0),
    )(*args)


def routing(ids_ref, experts):
    top, count = ids_ref.shape
    expert = lax.broadcasted_iota(jnp.int32, (experts, count), 0)
    matches = [expert == ids_ref[k : k + 1, :] for k in range(top)]
    picked = sum(m.astype(F32) for m in matches)
    earlier = lax.broadcasted_iota(jnp.int32, (count, count), 0) < lax.broadcasted_iota(
        jnp.int32, (count, count), 1
    )
    before = dot(picked.astype(BF), earlier.astype(F32).astype(BF))
    return jnp.where(picked > 0.0, before, -1.0), matches


def spread(per_expert):
    experts, count = per_expert.shape
    wide = jnp.broadcast_to(per_expert[:, None, :], (experts, MAIN, count))
    return wide.reshape(experts * MAIN, count)


def main_slots(slot):
    experts, count = slot.shape
    number = lax.broadcasted_iota(jnp.int32, (experts * MAIN, count), 0) % MAIN
    return spread(slot) == number.astype(F32)


def dispatch_kernel(ids_ref, weight_ref, tokens_ref, grads_ref, out_ref, packed):
    experts = out_ref.shape[0] // MAIN
    quarter = tokens_ref.shape[1]
    slot, matches = routing(ids_ref, experts)
    weight = sum(
        jnp.where(m, weight_ref[k : k + 1, :], 0.0) for k, m in enumerate(matches)
    )
    here = main_slots(slot)
    out_ref[:, :quarter] = dot(jnp.where(here, 1.0, 0.0).astype(BF), tokens_ref[...]).astype(BF)
    out_ref[:, quarter : 2 * quarter] = dot(
        jnp.where(here, spread(weight), 0.0).astype(BF), grads_ref[...]
    ).astype(BF)
    last = slot == float(MAIN)
    extra_tokens = dot(jnp.where(last, 1.0, 0.0).astype(BF), tokens_ref[...])
    extra_grads = dot(jnp.where(last, weight, 0.0).astype(BF), grads_ref[...])
    pieces = quarter // LANES
    for j in range(pieces):
        packed[:, j, :] = extra_tokens[:, j * LANES : (j + 1) * LANES]
        packed[:, pieces + j, :] = extra_grads[:, j * LANES : (j + 1) * LANES]
    out_ref[:, 2 * quarter :] = packed[...].reshape(experts * MAIN, LANES).astype(BF)


def expert_kernel(
    rows_ref, gate_ref, up_ref, down_ref, delta_ref, hidden_ref, back_ref, token_rows, grad_rows, packed
):
    groups, n, _ = rows_ref.shape
    quarter, ffw = gate_ref.shape[1:]
    m = n // MAIN
    pieces = quarter // LANES
    for q in range(groups):
        at = q * quarter
        token_rows[:n, at : at + quarter] = rows_ref[q, :, :quarter]
        grad_rows[:n, at : at + quarter] = rows_ref[q, :, quarter : 2 * quarter]
        packed[...] = rows_ref[q, :, 2 * quarter :].astype(F32).reshape(m, MAIN, LANES)
        for j in range(pieces):
            to = slice(at + j * LANES, at + (j + 1) * LANES)
            token_rows[n:, to] = packed[:, j, :].astype(BF)
            grad_rows[n:, to] = packed[:, pieces + j, :].astype(BF)
    full = (groups * quarter, ffw)
    gate = dot(token_rows[...], gate_ref[...].reshape(full))
    up = dot(token_rows[...], up_ref[...].reshape(full))
    back = sum(
        dot(grad_rows[:, q * quarter : (q + 1) * quarter], down_ref[q], CONTRACT_LAST)
        for q in range(groups)
    )
    sigmoid = 1.0 / (1.0 + jnp.exp(-gate))
    silu = gate * sigmoid
    hidden_ref[...] = (silu * up).astype(BF)
    gate_delta = (back * up * sigmoid * (1.0 + gate * (1.0 - sigmoid))).astype(BF)
    up_delta = (back * silu).astype(BF)
    delta_ref[:, :ffw] = gate_delta
    delta_ref[:, ffw:] = up_delta
    for j in range(pieces, MAIN):
        packed[:, j, :] = jnp.zeros((m, LANES), F32)
    for q in range(groups):
        out = dot(gate_delta, gate_ref[q], CONTRACT_LAST) + dot(up_delta, up_ref[q], CONTRACT_LAST)
        back_ref[q, :, :quarter] = out[:n, :].astype(BF)
        for j in range(pieces):
            packed[:, j, :] = out[n:, j * LANES : (j + 1) * LANES]
        back_ref[q, :, quarter:] = packed[...].reshape(n, LANES).astype(BF)


def row_blocks(rows_ref, packed, quarter, which):
    sources = rows_ref.shape[0] // MAIN
    pieces = quarter // LANES
    packed[...] = rows_ref[:, 2 * quarter :].astype(F32).reshape(sources, MAIN, LANES)
    n, m = rows_ref.shape[0] // 4, sources // 4
    columns = slice(which * quarter, (which + 1) * quarter)
    for r in range(4):
        extra = jnp.concatenate(
            [packed[r * m : (r + 1) * m, which * pieces + j, :] for j in range(pieces)], axis=1
        )
        yield r * (n + m), n, m, rows_ref[r * n : (r + 1) * n, columns], extra.astype(BF)


def token_weights_kernel(rows_ref, delta_ref, gate_ref, up_ref, packed):
    quarter, ffw = gate_ref.shape
    total = 0.0
    for at, n, m, rows, extra in row_blocks(rows_ref, packed, quarter, 0):
        total = total + dot(rows, delta_ref[at : at + n, :], CONTRACT_FIRST)
        total = total + dot(extra, delta_ref[at + n : at + n + m, :], CONTRACT_FIRST)
    gate_ref[...] = total[:, :ffw].astype(BF)
    up_ref[...] = total[:, ffw:].astype(BF)


def down_weights_kernel(rows_ref, hidden_ref, down_ref, packed):
    total = 0.0
    for at, n, m, rows, extra in row_blocks(rows_ref, packed, down_ref.shape[1], 1):
        total = total + dot(hidden_ref[at : at + n, :], rows, CONTRACT_FIRST)
        total = total + dot(hidden_ref[at + n : at + n + m, :], extra, CONTRACT_FIRST)
    down_ref[...] = total.astype(BF)


def combine_kernel(ids_ref, rows_ref, out_ref, packed):
    experts = rows_ref.shape[0] // MAIN
    quarter = out_ref.shape[1]
    slot, _ = routing(ids_ref, experts)
    here = jnp.where(main_slots(slot), 1.0, 0.0).astype(BF)
    last = jnp.where(slot == float(MAIN), 1.0, 0.0).astype(BF)
    packed[...] = rows_ref[:, quarter:].astype(F32).reshape(experts, MAIN, LANES)
    total = dot(here, rows_ref[:, :quarter], CONTRACT_FIRST)
    for j in range(quarter // LANES):
        at = slice(j * LANES, (j + 1) * LANES)
        extra = dot(last, packed[:, j, :].astype(BF), CONTRACT_FIRST)
        out_ref[:, at] = (total[:, at] + extra).astype(BF)


def exchange(blocks, axis):
    return lax.all_to_all(blocks, axis, split_axis=0, concat_axis=0, tiled=True)


def body(tokens, out_grad, expert_ids, route_weight, w_gate, w_up, w_down):
    experts = lax.axis_size("ep")
    groups = lax.axis_size("rep")
    count, quarter = tokens.shape
    ffw = w_gate.shape[2]
    main = experts * MAIN
    n, m = main // groups, experts // groups
    shape = jax.ShapeDtypeStruct
    packed = pltpu.VMEM((experts, MAIN, LANES), F32)

    gate_all, up_all, down_all = (
        lax.all_gather(w, "rep", axis=0, tiled=True) for w in (w_gate, w_up, w_down)
    )
    ids = expert_ids.T
    sent = kernel_call(
        dispatch_kernel,
        shape((main, 2 * quarter + LANES), BF),
        (ids, route_weight.T.astype(F32), tokens, out_grad),
        4 * main * count * quarter,
        (packed,),
    )
    rows = exchange(sent.reshape(experts, MAIN, -1), "ep").reshape(main, -1)
    wide_rows = exchange(rows.reshape(groups, n, -1), "rep")
    delta, hidden, back = kernel_call(
        expert_kernel,
        (
            shape((n + m, 2 * ffw), BF),
            shape((n + m, ffw), BF),
            shape((groups, n, quarter + LANES), BF),
        ),
        (wide_rows, gate_all, up_all, down_all),
        10 * (n + m) * groups * quarter * ffw,
        (
            pltpu.VMEM((n + m, groups * quarter), BF),
            pltpu.VMEM((n + m, groups * quarter), BF),
            pltpu.VMEM((m, MAIN, LANES), F32),
        ),
    )
    delta = lax.all_gather(delta, "rep", axis=0, tiled=True)
    hidden = lax.all_gather(hidden, "rep", axis=0, tiled=True)
    back = exchange(back, "rep")
    returned = exchange(back.reshape(experts, MAIN, -1), "ep").reshape(main, -1)
    grad_gate, grad_up = kernel_call(
        token_weights_kernel,
        (shape((quarter, ffw), BF), shape((quarter, ffw), BF)),
        (rows, delta),
        4 * (main + experts) * quarter * ffw,
        (packed,),
    )
    grad_down = kernel_call(
        down_weights_kernel,
        shape((ffw, quarter), BF),
        (rows, hidden),
        2 * (main + experts) * quarter * ffw,
        (packed,),
    )
    token_grad = kernel_call(
        combine_kernel,
        shape((count, quarter), BF),
        (ids, returned),
        2 * main * count * quarter,
        (packed,),
    )
    return token_grad, grad_gate[None], grad_up[None], grad_down[None]


def solution(mesh):
    rows = P("ep", "rep")
    by_width = P("ep", "rep", None)
    last = P("ep", None, "rep")
    return jax.shard_map(
        body,
        mesh=mesh,
        in_specs=(rows, rows, P("ep", None), P("ep", None), by_width, by_width, last),
        out_specs=(rows, by_width, by_width, last),
        check_vma=False,
    )
```

```python
import jax
import jax.numpy as jnp
from jax import lax
from jax.experimental import pallas as pl
from jax.experimental.pallas import tpu as pltpu
from jax.sharding import PartitionSpec as P

MAIN = 8
LANES = 128
BF = jnp.bfloat16
F32 = jnp.float32
CONTRACT_LAST = (((1,), (1,)), ((), ()))
CONTRACT_FIRST = (((0,), (0,)), ((), ()))


def dot(a, b, dims=(((1,), (0,)), ((), ()))):
    return lax.dot_general(a, b, dims, preferred_element_type=F32)


def kernel_call(body, out_shape, args, flops, scratch=(), in_hbm=()):
    moved = sum(a.size * a.dtype.itemsize for a in args)
    outs = out_shape if isinstance(out_shape, tuple) else (out_shape,)
    moved += sum(o.size * o.dtype.itemsize for o in outs)
    return pl.pallas_call(
        body,
        out_shape=out_shape,
        in_specs=[
            pl.BlockSpec(memory_space=pltpu.HBM if i in in_hbm else pltpu.VMEM)
            for i in range(len(args))
        ],
        out_specs=jax.tree.map(lambda _: pl.BlockSpec(memory_space=pltpu.VMEM), out_shape),
        scratch_shapes=list(scratch),
        compiler_params=pltpu.CompilerParams(vmem_limit_bytes=48 << 20),
        cost_estimate=pl.CostEstimate(flops=flops, bytes_accessed=moved, transcendentals=0),
    )(*args)


def routing(ids_ref, experts):
    top, count = ids_ref.shape
    expert = lax.broadcasted_iota(jnp.int32, (experts, count), 0)
    matches = [expert == ids_ref[k : k + 1, :] for k in range(top)]
    picked = sum(m.astype(F32) for m in matches)
    earlier = lax.broadcasted_iota(jnp.int32, (count, count), 0) < lax.broadcasted_iota(
        jnp.int32, (count, count), 1
    )
    before = dot(picked.astype(BF), earlier.astype(F32).astype(BF))
    return jnp.where(picked > 0.0, before, -1.0), matches


def spread(per_expert):
    experts, count = per_expert.shape
    wide = jnp.broadcast_to(per_expert[:, None, :], (experts, MAIN, count))
    return wide.reshape(experts * MAIN, count)


def main_slots(slot):
    experts, count = slot.shape
    number = lax.broadcasted_iota(jnp.int32, (experts * MAIN, count), 0) % MAIN
    return spread(slot) == number.astype(F32)


def pack_weights_kernel(gate_ref, up_ref, down_ref, out_ref):
    ffw = gate_ref.shape[1]
    out_ref[:, :ffw] = gate_ref[...]
    out_ref[:, ffw : 2 * ffw] = up_ref[...]
    out_ref[:, 2 * ffw :] = down_ref[...].T


def dispatch_kernel(
    ids_ref, weight_ref, tokens_hbm, grads_hbm, out_ref, packed, tokens_ref, grads_ref, sems
):
    loads = (
        pltpu.make_async_copy(tokens_hbm, tokens_ref, sems.at[0]),
        pltpu.make_async_copy(grads_hbm, grads_ref, sems.at[1]),
    )
    for load in loads:
        load.start()
    experts = out_ref.shape[0] // MAIN
    quarter = tokens_ref.shape[1]
    slot, matches = routing(ids_ref, experts)
    weight = sum(
        jnp.where(m, weight_ref[k : k + 1, :].astype(F32), 0.0) for k, m in enumerate(matches)
    )
    here = main_slots(slot)
    placing = jnp.where(here, 1.0, 0.0).astype(BF)
    weighing = jnp.where(here, spread(weight), 0.0).astype(BF)
    loads[0].wait()
    out_ref[:, :quarter] = dot(placing, tokens_ref[...]).astype(BF)
    loads[1].wait()
    out_ref[:, quarter : 2 * quarter] = dot(weighing, grads_ref[...]).astype(BF)
    last = slot == float(MAIN)
    extra_tokens = dot(jnp.where(last, 1.0, 0.0).astype(BF), tokens_ref[...])
    extra_grads = dot(jnp.where(last, weight, 0.0).astype(BF), grads_ref[...])
    pieces = quarter // LANES
    for j in range(pieces):
        packed[:, j, :] = extra_tokens[:, j * LANES : (j + 1) * LANES]
        packed[:, pieces + j, :] = extra_grads[:, j * LANES : (j + 1) * LANES]
    out_ref[:, 2 * quarter :] = packed[...].reshape(experts * MAIN, LANES).astype(BF)


def expert_kernel(rows_ref, weights_ref, terms_ref, back_ref, token_rows, grad_rows, packed):
    groups, n, _ = rows_ref.shape
    quarter = weights_ref.shape[1]
    ffw = weights_ref.shape[2] // 3
    m = n // MAIN
    pieces = quarter // LANES
    for q in range(groups):
        at = q * quarter
        token_rows[:n, at : at + quarter] = rows_ref[q, :, :quarter]
        grad_rows[:n, at : at + quarter] = rows_ref[q, :, quarter : 2 * quarter]
        packed[...] = rows_ref[q, :, 2 * quarter :].astype(F32).reshape(m, MAIN, LANES)
        for j in range(pieces):
            to = slice(at + j * LANES, at + (j + 1) * LANES)
            token_rows[n:, to] = packed[:, j, :].astype(BF)
            grad_rows[n:, to] = packed[:, pieces + j, :].astype(BF)

    def product(rows, part):
        weights = weights_ref[:, :, part * ffw : (part + 1) * ffw]
        return dot(rows[...], weights.reshape(groups * quarter, ffw))

    gate, up, back = product(token_rows, 0), product(token_rows, 1), product(grad_rows, 2)
    sigmoid = 1.0 / (1.0 + jnp.exp(-gate))
    silu = gate * sigmoid
    gate_delta = (back * up * sigmoid * (1.0 + gate * (1.0 - sigmoid))).astype(BF)
    up_delta = (back * silu).astype(BF)
    terms_ref[:, :ffw] = gate_delta
    terms_ref[:, ffw : 2 * ffw] = up_delta
    terms_ref[:, 2 * ffw :] = (silu * up).astype(BF)
    for j in range(pieces, MAIN):
        packed[:, j, :] = jnp.zeros((m, LANES), F32)
    for q in range(groups):
        out = dot(gate_delta, weights_ref[q, :, :ffw], CONTRACT_LAST)
        out = out + dot(up_delta, weights_ref[q, :, ffw : 2 * ffw], CONTRACT_LAST)
        back_ref[q, :, :quarter] = out[:n, :].astype(BF)
        for j in range(pieces):
            packed[:, j, :] = out[n:, j * LANES : (j + 1) * LANES]
        back_ref[q, :, quarter:] = packed[...].reshape(n, LANES).astype(BF)


def row_blocks(rows_ref, packed, quarter, which):
    sources = rows_ref.shape[0] // MAIN
    pieces = quarter // LANES
    packed[...] = rows_ref[:, 2 * quarter :].astype(F32).reshape(sources, MAIN, LANES)
    n, m = rows_ref.shape[0] // 4, sources // 4
    columns = slice(which * quarter, (which + 1) * quarter)
    for r in range(4):
        extra = jnp.concatenate(
            [packed[r * m : (r + 1) * m, which * pieces + j, :] for j in range(pieces)], axis=1
        )
        yield r * (n + m), n, m, rows_ref[r * n : (r + 1) * n, columns], extra.astype(BF)


def token_weights_kernel(rows_ref, terms_ref, gate_ref, up_ref, packed):
    quarter, ffw = gate_ref.shape
    total = 0.0
    for at, n, m, rows, extra in row_blocks(rows_ref, packed, quarter, 0):
        total = total + dot(rows, terms_ref[at : at + n, : 2 * ffw], CONTRACT_FIRST)
        total = total + dot(extra, terms_ref[at + n : at + n + m, : 2 * ffw], CONTRACT_FIRST)
    gate_ref[...] = total[:, :ffw].astype(BF)
    up_ref[...] = total[:, ffw:].astype(BF)


def down_weights_kernel(rows_ref, terms_ref, down_ref, packed):
    ffw, quarter = down_ref.shape
    total = 0.0
    for at, n, m, rows, extra in row_blocks(rows_ref, packed, quarter, 1):
        total = total + dot(terms_ref[at : at + n, 2 * ffw :], rows, CONTRACT_FIRST)
        total = total + dot(terms_ref[at + n : at + n + m, 2 * ffw :], extra, CONTRACT_FIRST)
    down_ref[...] = total.astype(BF)


def combine_kernel(ids_ref, rows_ref, out_ref, packed):
    experts = rows_ref.shape[0] // MAIN
    quarter = out_ref.shape[1]
    slot, _ = routing(ids_ref, experts)
    here = jnp.where(main_slots(slot), 1.0, 0.0).astype(BF)
    last = jnp.where(slot == float(MAIN), 1.0, 0.0).astype(BF)
    packed[...] = rows_ref[:, quarter:].astype(F32).reshape(experts, MAIN, LANES)
    total = dot(here, rows_ref[:, :quarter], CONTRACT_FIRST)
    for j in range(quarter // LANES):
        at = slice(j * LANES, (j + 1) * LANES)
        extra = dot(last, packed[:, j, :].astype(BF), CONTRACT_FIRST)
        out_ref[:, at] = (total[:, at] + extra).astype(BF)


def exchange(blocks, axis):
    return lax.all_to_all(blocks, axis, split_axis=0, concat_axis=0, tiled=True)


def body(tokens, out_grad, expert_ids, route_weight, w_gate, w_up, w_down):
    experts = lax.axis_size("ep")
    groups = lax.axis_size("rep")
    count, quarter = tokens.shape
    ffw = w_gate.shape[2]
    main = experts * MAIN
    n, m = main // groups, experts // groups
    shape = jax.ShapeDtypeStruct
    packed = pltpu.VMEM((experts, MAIN, LANES), F32)

    weights = kernel_call(
        pack_weights_kernel,
        shape((quarter, 3 * ffw), BF),
        (w_gate[0], w_up[0], w_down[0]),
        0,
    )
    weights = lax.all_gather(weights, "rep", axis=0)
    ids = expert_ids.T
    sent = kernel_call(
        dispatch_kernel,
        shape((main, 2 * quarter + LANES), BF),
        (ids, route_weight.T, tokens, out_grad),
        4 * main * count * quarter,
        (
            packed,
            pltpu.VMEM((count, quarter), BF),
            pltpu.VMEM((count, quarter), BF),
            pltpu.SemaphoreType.DMA((2,)),
        ),
        in_hbm=(2, 3),
    )
    rows = exchange(sent.reshape(experts, MAIN, -1), "ep").reshape(main, -1)
    wide_rows = exchange(rows.reshape(groups, n, -1), "rep")
    terms, back = kernel_call(
        expert_kernel,
        (shape((n + m, 3 * ffw), BF), shape((groups, n, quarter + LANES), BF)),
        (wide_rows, weights),
        10 * (n + m) * groups * quarter * ffw,
        (
            pltpu.VMEM((n + m, groups * quarter), BF),
            pltpu.VMEM((n + m, groups * quarter), BF),
            pltpu.VMEM((m, MAIN, LANES), F32),
        ),
    )
    terms = lax.all_gather(terms, "rep", axis=0, tiled=True)
    back = exchange(back, "rep")
    returned = exchange(back.reshape(experts, MAIN, -1), "ep").reshape(main, -1)
    grad_gate, grad_up = kernel_call(
        token_weights_kernel,
        (shape((quarter, ffw), BF), shape((quarter, ffw), BF)),
        (rows, terms),
        4 * (main + experts) * quarter * ffw,
        (packed,),
    )
    grad_down = kernel_call(
        down_weights_kernel,
        shape((ffw, quarter), BF),
        (rows, terms),
        2 * (main + experts) * quarter * ffw,
        (packed,),
    )
    token_grad = kernel_call(
        combine_kernel,
        shape((count, quarter), BF),
        (ids, returned),
        2 * main * count * quarter,
        (packed,),
    )
    return token_grad, grad_gate[None], grad_up[None], grad_down[None]


def solution(mesh):
    rows = P("ep", "rep")
    by_width = P("ep", "rep", None)
    last = P("ep", None, "rep")
    return jax.shard_map(
        body,
        mesh=mesh,
        in_specs=(rows, rows, P("ep", None), P("ep", None), by_width, by_width, last),
        out_specs=(rows, by_width, by_width, last),
        check_vma=False,
    )
```

```python
import jax
import jax.numpy as jnp
from jax import lax
from jax.experimental import pallas as pl
from jax.experimental.pallas import tpu as pltpu
from jax.sharding import PartitionSpec as P

MAIN = 8
LANES = 128
BF = jnp.bfloat16
F32 = jnp.float32
CONTRACT_LAST = (((1,), (1,)), ((), ()))
CONTRACT_FIRST = (((0,), (0,)), ((), ()))


def dot(a, b, dims=(((1,), (0,)), ((), ()))):
    return lax.dot_general(a, b, dims, preferred_element_type=F32)


def kernel_call(body, out_shape, args, flops, scratch=(), in_hbm=(), vmem=48):
    moved = sum(a.size * a.dtype.itemsize for a in args)
    outs = out_shape if isinstance(out_shape, tuple) else (out_shape,)
    moved += sum(o.size * o.dtype.itemsize for o in outs)
    return pl.pallas_call(
        body,
        out_shape=out_shape,
        in_specs=[
            pl.BlockSpec(memory_space=pl.ANY if i in in_hbm else pltpu.VMEM)
            for i in range(len(args))
        ],
        out_specs=jax.tree.map(lambda _: pl.BlockSpec(memory_space=pltpu.VMEM), out_shape),
        scratch_shapes=list(scratch),
        compiler_params=pltpu.CompilerParams(vmem_limit_bytes=vmem << 20),
        cost_estimate=pl.CostEstimate(flops=flops, bytes_accessed=moved, transcendentals=0),
    )(*args)


def routing(ids_ref, experts):
    top, count = ids_ref.shape
    expert = lax.broadcasted_iota(jnp.int32, (experts, count), 0)
    matches = [expert == ids_ref[k : k + 1, :] for k in range(top)]
    picked = sum(m.astype(F32) for m in matches)
    earlier = lax.broadcasted_iota(jnp.int32, (count, count), 0) < lax.broadcasted_iota(
        jnp.int32, (count, count), 1
    )
    before = dot(picked.astype(BF), earlier.astype(F32).astype(BF))
    return jnp.where(picked > 0.0, before, -1.0), matches


def spread(per_expert):
    experts, count = per_expert.shape
    wide = jnp.broadcast_to(per_expert[:, None, :], (experts, MAIN, count))
    return wide.reshape(experts * MAIN, count)


def main_slots(slot):
    experts, count = slot.shape
    number = lax.broadcasted_iota(jnp.int32, (experts * MAIN, count), 0) % MAIN
    return spread(slot) == number.astype(F32)


def pack_weights_kernel(gate_ref, up_ref, down_ref, out_ref):
    ffw = gate_ref.shape[1]
    out_ref[:, :ffw] = gate_ref[...]
    out_ref[:, ffw : 2 * ffw] = up_ref[...]
    out_ref[:, 2 * ffw :] = down_ref[...].T


def dispatch_kernel(
    ids_ref, weight_ref, tokens_hbm, grads_hbm, out_ref, packed, tokens_ref, grads_ref, sems
):
    loads = (
        pltpu.make_async_copy(tokens_hbm, tokens_ref, sems.at[0]),
        pltpu.make_async_copy(grads_hbm, grads_ref, sems.at[1]),
    )
    for load in loads:
        load.start()
    experts = out_ref.shape[0] // MAIN
    quarter = tokens_ref.shape[1]
    slot, matches = routing(ids_ref, experts)
    weight = sum(
        jnp.where(m, weight_ref[k : k + 1, :].astype(F32), 0.0) for k, m in enumerate(matches)
    )
    here = main_slots(slot)
    placing = jnp.where(here, 1.0, 0.0).astype(BF)
    weighing = jnp.where(here, spread(weight), 0.0).astype(BF)
    loads[0].wait()
    out_ref[:, :quarter] = dot(placing, tokens_ref[...]).astype(BF)
    loads[1].wait()
    out_ref[:, quarter : 2 * quarter] = dot(weighing, grads_ref[...]).astype(BF)
    last = slot == float(MAIN)
    extra_tokens = dot(jnp.where(last, 1.0, 0.0).astype(BF), tokens_ref[...])
    extra_grads = dot(jnp.where(last, weight, 0.0).astype(BF), grads_ref[...])
    pieces = quarter // LANES
    for j in range(pieces):
        packed[:, j, :] = extra_tokens[:, j * LANES : (j + 1) * LANES]
        packed[:, pieces + j, :] = extra_grads[:, j * LANES : (j + 1) * LANES]
    out_ref[:, 2 * quarter :] = packed[...].reshape(experts * MAIN, LANES).astype(BF)


def expert_kernel(
    rows_hbm, weights_hbm, terms_ref, back_ref, rows_ref, weights_ref, packed, row_sems, weight_sems
):
    groups, n, _ = rows_ref.shape
    quarter = weights_ref.shape[1]
    ffw = weights_ref.shape[2] // 3
    m = n // MAIN
    pieces = quarter // LANES
    loads = []
    for q in range(groups):
        rows = pltpu.make_async_copy(rows_hbm.at[q], rows_ref.at[q], row_sems.at[q])
        weights = pltpu.make_async_copy(weights_hbm.at[q], weights_ref.at[q], weight_sems.at[q])
        rows.start()
        weights.start()
        loads.append((rows, weights))

    gate, up, back = 0.0, 0.0, 0.0
    for q, (rows, weights) in enumerate(loads):
        rows.wait()
        packed[...] = rows_ref[q, :, 2 * quarter :].astype(F32).reshape(m, MAIN, LANES)
        extra = [packed[:, j, :].astype(BF) for j in range(2 * pieces)]
        token_rows = jnp.concatenate(
            [rows_ref[q, :, :quarter], jnp.concatenate(extra[:pieces], axis=1)], axis=0
        )
        grad_rows = jnp.concatenate(
            [rows_ref[q, :, quarter : 2 * quarter], jnp.concatenate(extra[pieces:], axis=1)], axis=0
        )
        weights.wait()
        gate = gate + dot(token_rows, weights_ref[q, :, :ffw])
        up = up + dot(token_rows, weights_ref[q, :, ffw : 2 * ffw])
        back = back + dot(grad_rows, weights_ref[q, :, 2 * ffw :])
    sigmoid = 1.0 / (1.0 + jnp.exp(-gate))
    silu = gate * sigmoid
    gate_delta = (back * up * sigmoid * (1.0 + gate * (1.0 - sigmoid))).astype(BF)
    up_delta = (back * silu).astype(BF)
    terms_ref[:, :ffw] = gate_delta
    terms_ref[:, ffw : 2 * ffw] = up_delta
    terms_ref[:, 2 * ffw :] = (silu * up).astype(BF)
    for j in range(pieces, MAIN):
        packed[:, j, :] = jnp.zeros((m, LANES), F32)
    for q in range(groups):
        out = dot(gate_delta, weights_ref[q, :, :ffw], CONTRACT_LAST)
        out = out + dot(up_delta, weights_ref[q, :, ffw : 2 * ffw], CONTRACT_LAST)
        back_ref[q, :, :quarter] = out[:n, :].astype(BF)
        for j in range(pieces):
            packed[:, j, :] = out[n:, j * LANES : (j + 1) * LANES]
        back_ref[q, :, quarter:] = packed[...].reshape(n, LANES).astype(BF)


def row_blocks(rows_ref, packed, quarter, which):
    sources = rows_ref.shape[0] // MAIN
    pieces = quarter // LANES
    packed[...] = rows_ref[:, 2 * quarter :].astype(F32).reshape(sources, MAIN, LANES)
    n, m = rows_ref.shape[0] // 4, sources // 4
    columns = slice(which * quarter, (which + 1) * quarter)
    for r in range(4):
        extra = jnp.concatenate(
            [packed[r * m : (r + 1) * m, which * pieces + j, :] for j in range(pieces)], axis=1
        )
        yield r * (n + m), n, m, rows_ref[r * n : (r + 1) * n, columns], extra.astype(BF)


def token_weights_kernel(rows_ref, terms_ref, gate_ref, up_ref, packed):
    quarter, ffw = gate_ref.shape
    total = 0.0
    for at, n, m, rows, extra in row_blocks(rows_ref, packed, quarter, 0):
        total = total + dot(rows, terms_ref[at : at + n, : 2 * ffw], CONTRACT_FIRST)
        total = total + dot(extra, terms_ref[at + n : at + n + m, : 2 * ffw], CONTRACT_FIRST)
    gate_ref[...] = total[:, :ffw].astype(BF)
    up_ref[...] = total[:, ffw:].astype(BF)


def down_weights_kernel(rows_ref, terms_ref, down_ref, packed):
    ffw, quarter = down_ref.shape
    total = 0.0
    for at, n, m, rows, extra in row_blocks(rows_ref, packed, quarter, 1):
        total = total + dot(terms_ref[at : at + n, 2 * ffw :], rows, CONTRACT_FIRST)
        total = total + dot(terms_ref[at + n : at + n + m, 2 * ffw :], extra, CONTRACT_FIRST)
    down_ref[...] = total.astype(BF)


def combine_kernel(ids_ref, rows_ref, out_ref, packed):
    experts = rows_ref.shape[0] // MAIN
    quarter = out_ref.shape[1]
    slot, _ = routing(ids_ref, experts)
    here = jnp.where(main_slots(slot), 1.0, 0.0).astype(BF)
    last = jnp.where(slot == float(MAIN), 1.0, 0.0).astype(BF)
    packed[...] = rows_ref[:, quarter:].astype(F32).reshape(experts, MAIN, LANES)
    total = dot(here, rows_ref[:, :quarter], CONTRACT_FIRST)
    for j in range(quarter // LANES):
        at = slice(j * LANES, (j + 1) * LANES)
        extra = dot(last, packed[:, j, :].astype(BF), CONTRACT_FIRST)
        out_ref[:, at] = (total[:, at] + extra).astype(BF)


def exchange(blocks, axis):
    return lax.all_to_all(blocks, axis, split_axis=0, concat_axis=0, tiled=True)


def body(tokens, out_grad, expert_ids, route_weight, w_gate, w_up, w_down):
    experts = lax.axis_size("ep")
    groups = lax.axis_size("rep")
    count, quarter = tokens.shape
    ffw = w_gate.shape[2]
    main = experts * MAIN
    n, m = main // groups, experts // groups
    shape = jax.ShapeDtypeStruct
    packed = pltpu.VMEM((experts, MAIN, LANES), F32)

    weights = kernel_call(
        pack_weights_kernel,
        shape((quarter, 3 * ffw), BF),
        (w_gate[0], w_up[0], w_down[0]),
        0,
        vmem=60,
    )
    weights = lax.all_gather(weights, "rep", axis=0)
    ids = expert_ids.T
    sent = kernel_call(
        dispatch_kernel,
        shape((main, 2 * quarter + LANES), BF),
        (ids, route_weight.T, tokens, out_grad),
        4 * main * count * quarter,
        (
            packed,
            pltpu.VMEM((count, quarter), BF),
            pltpu.VMEM((count, quarter), BF),
            pltpu.SemaphoreType.DMA((2,)),
        ),
        in_hbm=(2, 3),
    )
    rows = exchange(sent.reshape(experts, MAIN, -1), "ep").reshape(main, -1)
    wide_rows = exchange(rows.reshape(groups, n, -1), "rep")
    terms, back = kernel_call(
        expert_kernel,
        (shape((n + m, 3 * ffw), BF), shape((groups, n, quarter + LANES), BF)),
        (wide_rows, weights),
        10 * (n + m) * groups * quarter * ffw,
        (
            pltpu.VMEM((groups, n, 2 * quarter + LANES), BF),
            pltpu.VMEM((groups, quarter, 3 * ffw), BF),
            pltpu.VMEM((m, MAIN, LANES), F32),
            pltpu.SemaphoreType.DMA((groups,)),
            pltpu.SemaphoreType.DMA((groups,)),
        ),
        in_hbm=(0, 1),
        vmem=60,
    )
    terms = lax.all_gather(terms, "rep", axis=0, tiled=True)
    back = exchange(back, "rep")
    returned = exchange(back.reshape(experts, MAIN, -1), "ep").reshape(main, -1)
    grad_gate, grad_up = kernel_call(
        token_weights_kernel,
        (shape((quarter, ffw), BF), shape((quarter, ffw), BF)),
        (rows, terms),
        4 * (main + experts) * quarter * ffw,
        (packed,),
    )
    grad_down = kernel_call(
        down_weights_kernel,
        shape((ffw, quarter), BF),
        (rows, terms),
        2 * (main + experts) * quarter * ffw,
        (packed,),
    )
    ids, grad_gate, grad_up, grad_down = lax.optimization_barrier(
        (ids, grad_gate, grad_up, grad_down)
    )
    token_grad = kernel_call(
        combine_kernel,
        shape((count, quarter), BF),
        (ids, returned),
        2 * main * count * quarter,
        (packed,),
    )
    return token_grad, grad_gate[None], grad_up[None], grad_down[None]


def solution(mesh):
    rows = P("ep", "rep")
    by_width = P("ep", "rep", None)
    last = P("ep", None, "rep")
    return jax.shard_map(
        body,
        mesh=mesh,
        in_specs=(rows, rows, P("ep", None), P("ep", None), by_width, by_width, last),
        out_specs=(rows, by_width, by_width, last),
        check_vma=False,
    )
```

```python
import jax
import jax.numpy as jnp
from jax import lax
from jax.experimental import pallas as pl
from jax.experimental.pallas import tpu as pltpu
from jax.sharding import PartitionSpec as P

MAIN = 8
LANES = 128
BF = jnp.bfloat16
F32 = jnp.float32
CONTRACT_LAST = (((1,), (1,)), ((), ()))
CONTRACT_FIRST = (((0,), (0,)), ((), ()))


def dot(a, b, dims=(((1,), (0,)), ((), ()))):
    return lax.dot_general(a, b, dims, preferred_element_type=F32)


def kernel_call(body, out_shape, args, flops, scratch=(), in_hbm=(), in_smem=(), out_hbm=False, vmem=48):
    moved = sum(a.size * a.dtype.itemsize for a in args)
    outs = out_shape if isinstance(out_shape, tuple) else (out_shape,)
    moved += sum(o.size * o.dtype.itemsize for o in outs)
    return pl.pallas_call(
        body,
        out_shape=out_shape,
        in_specs=[
            pl.BlockSpec(
                memory_space=pl.ANY if i in in_hbm else pltpu.SMEM if i in in_smem else pltpu.VMEM
            )
            for i in range(len(args))
        ],
        out_specs=jax.tree.map(
            lambda _: pl.BlockSpec(memory_space=pl.ANY if out_hbm else pltpu.VMEM), out_shape
        ),
        scratch_shapes=list(scratch),
        compiler_params=pltpu.CompilerParams(vmem_limit_bytes=vmem << 20),
        cost_estimate=pl.CostEstimate(flops=flops, bytes_accessed=moved, transcendentals=0),
    )(*args)


def routing(ids_ref, experts):
    top, count = ids_ref.shape
    expert = lax.broadcasted_iota(jnp.int32, (experts, count), 0)
    matches = [expert == ids_ref[k : k + 1, :] for k in range(top)]
    picked = sum(m.astype(F32) for m in matches)
    earlier = lax.broadcasted_iota(jnp.int32, (count, count), 0) < lax.broadcasted_iota(
        jnp.int32, (count, count), 1
    )
    before = dot(picked.astype(BF), earlier.astype(F32).astype(BF))
    return jnp.where(picked > 0.0, before, -1.0), matches


def spread(per_expert):
    experts, count = per_expert.shape
    wide = jnp.broadcast_to(per_expert[:, None, :], (experts, MAIN, count))
    return wide.reshape(experts * MAIN, count)


def main_slots(slot):
    experts, count = slot.shape
    number = lax.broadcasted_iota(jnp.int32, (experts * MAIN, count), 0) % MAIN
    return spread(slot) == number.astype(F32)


def pack_weights_kernel(gate_hbm, up_hbm, out_hbm, sems):
    ffw = gate_hbm.shape[1]
    copies = (
        pltpu.make_async_copy(gate_hbm, out_hbm.at[:, :ffw], sems.at[0]),
        pltpu.make_async_copy(up_hbm, out_hbm.at[:, ffw:], sems.at[1]),
    )
    for copy in copies:
        copy.start()
    for copy in copies:
        copy.wait()


def dispatch_kernel(
    ids_ref, weight_ref, tokens_hbm, grads_hbm, out_ref, packed, tokens_ref, grads_ref, sems
):
    loads = (
        pltpu.make_async_copy(tokens_hbm, tokens_ref, sems.at[0]),
        pltpu.make_async_copy(grads_hbm, grads_ref, sems.at[1]),
    )
    for load in loads:
        load.start()
    experts = out_ref.shape[0] // MAIN
    quarter = tokens_ref.shape[1]
    slot, matches = routing(ids_ref, experts)
    weight = sum(
        jnp.where(m, weight_ref[k : k + 1, :].astype(F32), 0.0) for k, m in enumerate(matches)
    )
    here = main_slots(slot)
    placing = jnp.where(here, 1.0, 0.0).astype(BF)
    weighing = jnp.where(here, spread(weight), 0.0).astype(BF)
    loads[0].wait()
    out_ref[:, :quarter] = dot(placing, tokens_ref[...]).astype(BF)
    loads[1].wait()
    out_ref[:, quarter : 2 * quarter] = dot(weighing, grads_ref[...]).astype(BF)
    last = slot == float(MAIN)
    extra_tokens = dot(jnp.where(last, 1.0, 0.0).astype(BF), tokens_ref[...])
    extra_grads = dot(jnp.where(last, weight, 0.0).astype(BF), grads_ref[...])
    pieces = quarter // LANES
    for j in range(pieces):
        packed[:, j, :] = extra_tokens[:, j * LANES : (j + 1) * LANES]
        packed[:, pieces + j, :] = extra_grads[:, j * LANES : (j + 1) * LANES]
    out_ref[:, 2 * quarter :] = packed[...].reshape(experts * MAIN, LANES).astype(BF)


def expert_kernel(
    rank_ref, rows_hbm, weights_hbm, *refs
):
    *downs_hbm, terms_ref, back_ref, rows_ref, weights_ref, downs_ref, grad_rows, packed, sems = refs
    groups, n, _ = rows_ref.shape
    quarter = weights_ref.shape[1]
    ffw = weights_ref.shape[2] // 2
    m = n // MAIN
    pieces = quarter // LANES
    loads = []
    for q in range(groups):
        load = (
            pltpu.make_async_copy(rows_hbm.at[q], rows_ref.at[q], sems.at[0, q]),
            pltpu.make_async_copy(weights_hbm.at[q], weights_ref.at[q], sems.at[1, q]),
        )
        load[0].start()
        load[1].start()
        loads.append(load)
    down_loads = [
        pltpu.make_async_copy(downs_hbm[k], downs_ref.at[k], sems.at[2, k]) for k in range(groups)
    ]
    for load in down_loads:
        load.start()

    gate, up, back = 0.0, 0.0, 0.0
    for q, (rows, weights) in enumerate(loads):
        rows.wait()
        packed[...] = rows_ref[q, :, 2 * quarter :].astype(F32).reshape(m, MAIN, LANES)
        extra = [packed[:, j, :].astype(BF) for j in range(2 * pieces)]
        token_rows = jnp.concatenate(
            [rows_ref[q, :, :quarter], jnp.concatenate(extra[:pieces], axis=1)], axis=0
        )
        grad_rows[q, :n, :] = rows_ref[q, :, quarter : 2 * quarter]
        grad_rows[q, n:, :] = jnp.concatenate(extra[pieces:], axis=1)
        weights.wait()
        gate = gate + dot(token_rows, weights_ref[q, :, :ffw])
        up = up + dot(token_rows, weights_ref[q, :, ffw:])
    for k, load in enumerate(down_loads):
        load.wait()
        source = lax.rem(rank_ref[0] - k + groups, groups)
        back = back + dot(grad_rows[source], downs_ref[k], CONTRACT_LAST)
    sigmoid = 1.0 / (1.0 + jnp.exp(-gate))
    silu = gate * sigmoid
    gate_delta = (back * up * sigmoid * (1.0 + gate * (1.0 - sigmoid))).astype(BF)
    up_delta = (back * silu).astype(BF)
    terms_ref[:, :ffw] = gate_delta
    terms_ref[:, ffw : 2 * ffw] = up_delta
    terms_ref[:, 2 * ffw :] = (silu * up).astype(BF)
    for j in range(pieces, MAIN):
        packed[:, j, :] = jnp.zeros((m, LANES), F32)
    for q in range(groups):
        out = dot(gate_delta, weights_ref[q, :, :ffw], CONTRACT_LAST)
        out = out + dot(up_delta, weights_ref[q, :, ffw:], CONTRACT_LAST)
        back_ref[q, :, :quarter] = out[:n, :].astype(BF)
        for j in range(pieces):
            packed[:, j, :] = out[n:, j * LANES : (j + 1) * LANES]
        back_ref[q, :, quarter:] = packed[...].reshape(n, LANES).astype(BF)


def row_blocks(rows_ref, packed, quarter, which):
    sources = rows_ref.shape[0] // MAIN
    pieces = quarter // LANES
    packed[...] = rows_ref[:, 2 * quarter :].astype(F32).reshape(sources, MAIN, LANES)
    n, m = rows_ref.shape[0] // 4, sources // 4
    columns = slice(which * quarter, (which + 1) * quarter)
    for r in range(4):
        extra = jnp.concatenate(
            [packed[r * m : (r + 1) * m, which * pieces + j, :] for j in range(pieces)], axis=1
        )
        yield r * (n + m), n, m, rows_ref[r * n : (r + 1) * n, columns], extra.astype(BF)


def token_weights_kernel(rows_ref, terms_ref, gate_ref, up_ref, packed):
    quarter, ffw = gate_ref.shape
    total = 0.0
    for at, n, m, rows, extra in row_blocks(rows_ref, packed, quarter, 0):
        total = total + dot(rows, terms_ref[at : at + n, : 2 * ffw], CONTRACT_FIRST)
        total = total + dot(extra, terms_ref[at + n : at + n + m, : 2 * ffw], CONTRACT_FIRST)
    gate_ref[...] = total[:, :ffw].astype(BF)
    up_ref[...] = total[:, ffw:].astype(BF)


def down_weights_kernel(rows_ref, terms_ref, down_ref, packed):
    ffw, quarter = down_ref.shape
    total = 0.0
    for at, n, m, rows, extra in row_blocks(rows_ref, packed, quarter, 1):
        total = total + dot(terms_ref[at : at + n, 2 * ffw :], rows, CONTRACT_FIRST)
        total = total + dot(terms_ref[at + n : at + n + m, 2 * ffw :], extra, CONTRACT_FIRST)
    down_ref[...] = total.astype(BF)


def combine_kernel(ids_ref, rows_ref, out_ref, packed):
    experts = rows_ref.shape[0] // MAIN
    quarter = out_ref.shape[1]
    slot, _ = routing(ids_ref, experts)
    here = jnp.where(main_slots(slot), 1.0, 0.0).astype(BF)
    last = jnp.where(slot == float(MAIN), 1.0, 0.0).astype(BF)
    packed[...] = rows_ref[:, quarter:].astype(F32).reshape(experts, MAIN, LANES)
    total = dot(here, rows_ref[:, :quarter], CONTRACT_FIRST)
    for j in range(quarter // LANES):
        at = slice(j * LANES, (j + 1) * LANES)
        extra = dot(last, packed[:, j, :].astype(BF), CONTRACT_FIRST)
        out_ref[:, at] = (total[:, at] + extra).astype(BF)


def exchange(blocks, axis):
    return lax.all_to_all(blocks, axis, split_axis=0, concat_axis=0, tiled=True)


def body(tokens, out_grad, expert_ids, route_weight, w_gate, w_up, w_down):
    experts = lax.axis_size("ep")
    groups = lax.axis_size("rep")
    count, quarter = tokens.shape
    ffw = w_gate.shape[2]
    main = experts * MAIN
    n, m = main // groups, experts // groups
    shape = jax.ShapeDtypeStruct
    packed = pltpu.VMEM((experts, MAIN, LANES), F32)

    weights = kernel_call(
        pack_weights_kernel,
        shape((quarter, 2 * ffw), BF),
        (w_gate[0], w_up[0]),
        0,
        (pltpu.SemaphoreType.DMA((2,)),),
        in_hbm=(0, 1),
        out_hbm=True,
        vmem=60,
    )
    weights = lax.all_gather(weights, "rep", axis=0)
    ids = expert_ids.T
    sent = kernel_call(
        dispatch_kernel,
        shape((main, 2 * quarter + LANES), BF),
        (ids, route_weight.T, tokens, out_grad),
        4 * main * count * quarter,
        (
            packed,
            pltpu.VMEM((count, quarter), BF),
            pltpu.VMEM((count, quarter), BF),
            pltpu.SemaphoreType.DMA((2,)),
        ),
        in_hbm=(2, 3),
    )
    down, sent = lax.optimization_barrier((w_down[0], sent))
    downs = [down] + [
        lax.ppermute(down, "rep", [(i, (i + k) % groups) for i in range(groups)])
        for k in range(1, groups)
    ]
    rows = exchange(sent.reshape(experts, MAIN, -1), "ep").reshape(main, -1)
    rows, *downs = lax.optimization_barrier((rows, *downs))
    wide_rows = exchange(rows.reshape(groups, n, -1), "rep")
    terms, back = kernel_call(
        expert_kernel,
        (shape((n + m, 3 * ffw), BF), shape((groups, n, quarter + LANES), BF)),
        (lax.axis_index("rep").astype(jnp.int32).reshape(1), wide_rows, weights, *downs),
        10 * (n + m) * groups * quarter * ffw,
        (
            pltpu.VMEM((groups, n, 2 * quarter + LANES), BF),
            pltpu.VMEM((groups, quarter, 2 * ffw), BF),
            pltpu.VMEM((groups, ffw, quarter), BF),
            pltpu.VMEM((groups, n + m, quarter), BF),
            pltpu.VMEM((m, MAIN, LANES), F32),
            pltpu.SemaphoreType.DMA((3, groups)),
        ),
        in_smem=(0,),
        in_hbm=range(1, 3 + groups),
        vmem=60,
    )
    terms = lax.all_gather(terms, "rep", axis=0, tiled=True)
    back = exchange(back, "rep")
    returned = exchange(back.reshape(experts, MAIN, -1), "ep").reshape(main, -1)
    grad_gate, grad_up = kernel_call(
        token_weights_kernel,
        (shape((quarter, ffw), BF), shape((quarter, ffw), BF)),
        (rows, terms),
        4 * (main + experts) * quarter * ffw,
        (packed,),
    )
    grad_down = kernel_call(
        down_weights_kernel,
        shape((ffw, quarter), BF),
        (rows, terms),
        2 * (main + experts) * quarter * ffw,
        (packed,),
    )
    ids, grad_gate, grad_up, grad_down = lax.optimization_barrier(
        (ids, grad_gate, grad_up, grad_down)
    )
    token_grad = kernel_call(
        combine_kernel,
        shape((count, quarter), BF),
        (ids, returned),
        2 * main * count * quarter,
        (packed,),
    )
    return token_grad, grad_gate[None], grad_up[None], grad_down[None]


def solution(mesh):
    rows = P("ep", "rep")
    by_width = P("ep", "rep", None)
    last = P("ep", None, "rep")
    return jax.shard_map(
        body,
        mesh=mesh,
        in_specs=(rows, rows, P("ep", None), P("ep", None), by_width, by_width, last),
        out_specs=(rows, by_width, by_width, last),
        check_vma=False,
    )
```

```python
import jax
import jax.numpy as jnp
from jax import lax
from jax.experimental import pallas as pl
from jax.experimental.pallas import tpu as pltpu
from jax.sharding import PartitionSpec as P

MAIN = 8
LANES = 128
BF = jnp.bfloat16
F32 = jnp.float32
CONTRACT_LAST = (((1,), (1,)), ((), ()))
CONTRACT_FIRST = (((0,), (0,)), ((), ()))


def dot(a, b, dims=(((1,), (0,)), ((), ()))):
    return lax.dot_general(a, b, dims, preferred_element_type=F32)


def kernel_call(body, out_shape, args, flops, scratch=(), in_hbm=(), vmem=48):
    moved = sum(a.size * a.dtype.itemsize for a in args)
    outs = out_shape if isinstance(out_shape, tuple) else (out_shape,)
    moved += sum(o.size * o.dtype.itemsize for o in outs)
    return pl.pallas_call(
        body,
        out_shape=out_shape,
        in_specs=[
            pl.BlockSpec(memory_space=pl.ANY if i in in_hbm else pltpu.VMEM)
            for i in range(len(args))
        ],
        out_specs=jax.tree.map(lambda _: pl.BlockSpec(memory_space=pltpu.VMEM), out_shape),
        scratch_shapes=list(scratch),
        compiler_params=pltpu.CompilerParams(vmem_limit_bytes=vmem << 20),
        cost_estimate=pl.CostEstimate(flops=flops, bytes_accessed=moved, transcendentals=0),
    )(*args)


def routing(ids_ref, experts):
    top, count = ids_ref.shape
    expert = lax.broadcasted_iota(jnp.int32, (experts, count), 0)
    matches = [expert == ids_ref[k : k + 1, :] for k in range(top)]
    picked = sum(m.astype(F32) for m in matches)
    earlier = lax.broadcasted_iota(jnp.int32, (count, count), 0) < lax.broadcasted_iota(
        jnp.int32, (count, count), 1
    )
    before = dot(picked.astype(BF), earlier.astype(F32).astype(BF))
    return jnp.where(picked > 0.0, before, -1.0), matches


def spread(per_expert):
    experts, count = per_expert.shape
    wide = jnp.broadcast_to(per_expert[:, None, :], (experts, MAIN, count))
    return wide.reshape(experts * MAIN, count)


def main_slots(slot):
    experts, count = slot.shape
    number = lax.broadcasted_iota(jnp.int32, (experts * MAIN, count), 0) % MAIN
    return spread(slot) == number.astype(F32)


def pack_weights_kernel(gate_ref, up_ref, out_ref):
    ffw = gate_ref.shape[1]
    out_ref[:, :ffw] = gate_ref[...]
    out_ref[:, ffw:] = up_ref[...]


def dispatch_kernel(
    ids_ref, weight_ref, tokens_hbm, grads_hbm, out_ref, packed, tokens_ref, grads_ref, sems
):
    loads = (
        pltpu.make_async_copy(tokens_hbm, tokens_ref, sems.at[0]),
        pltpu.make_async_copy(grads_hbm, grads_ref, sems.at[1]),
    )
    for load in loads:
        load.start()
    experts = out_ref.shape[0] // MAIN
    quarter = tokens_ref.shape[1]
    slot, matches = routing(ids_ref, experts)
    weight = sum(
        jnp.where(m, weight_ref[k : k + 1, :].astype(F32), 0.0) for k, m in enumerate(matches)
    )
    here = main_slots(slot)
    placing = jnp.where(here, 1.0, 0.0).astype(BF)
    weighing = jnp.where(here, spread(weight), 0.0).astype(BF)
    loads[0].wait()
    out_ref[:, :quarter] = dot(placing, tokens_ref[...]).astype(BF)
    loads[1].wait()
    out_ref[:, quarter + LANES :] = dot(weighing, grads_ref[...]).astype(BF)
    last = slot == float(MAIN)
    extra_tokens = dot(jnp.where(last, 1.0, 0.0).astype(BF), tokens_ref[...])
    extra_grads = dot(jnp.where(last, weight, 0.0).astype(BF), grads_ref[...])
    pieces = quarter // LANES
    for j in range(pieces):
        packed[:, j, :] = extra_tokens[:, j * LANES : (j + 1) * LANES]
        packed[:, pieces + j, :] = extra_grads[:, j * LANES : (j + 1) * LANES]
    out_ref[:, quarter : quarter + LANES] = (
        packed[...].reshape(experts * MAIN, LANES).astype(BF)
    )


def grad_products_kernel(rows_ref, down_ref, out_ref, packed):
    quarter = down_ref.shape[1]
    for at, n, m, rows, extra in row_blocks(rows_ref, packed, quarter, 1):
        out_ref[at : at + n, :] = dot(rows, down_ref[...], CONTRACT_LAST).astype(BF)
        out_ref[at + n : at + n + m, :] = dot(extra, down_ref[...], CONTRACT_LAST).astype(BF)


def expert_kernel(
    rows_hbm, weights_hbm, back_hbm, terms_ref, out_back_ref, rows_ref, weights_ref, back_ref, packed, sems
):
    groups, n, _ = rows_ref.shape
    quarter = weights_ref.shape[1]
    ffw = weights_ref.shape[2] // 2
    m = n // MAIN
    pieces = quarter // LANES
    loads = []
    for q in range(groups):
        load = (
            pltpu.make_async_copy(rows_hbm.at[q], rows_ref.at[q], sems.at[0, q]),
            pltpu.make_async_copy(weights_hbm.at[q], weights_ref.at[q], sems.at[1, q]),
        )
        load[0].start()
        load[1].start()
        loads.append(load)
    back_load = pltpu.make_async_copy(back_hbm, back_ref, sems.at[0, groups])
    back_load.start()

    gate, up = 0.0, 0.0
    for q, (rows, weights) in enumerate(loads):
        rows.wait()
        packed[...] = rows_ref[q, :, quarter:].astype(F32).reshape(m, MAIN, LANES)
        extra = [packed[:, j, :].astype(BF) for j in range(pieces)]
        token_rows = jnp.concatenate(
            [rows_ref[q, :, :quarter], jnp.concatenate(extra, axis=1)], axis=0
        )
        weights.wait()
        gate = gate + dot(token_rows, weights_ref[q, :, :ffw])
        up = up + dot(token_rows, weights_ref[q, :, ffw:])
    back_load.wait()
    back = back_ref[...].astype(F32)
    sigmoid = 1.0 / (1.0 + jnp.exp(-gate))
    silu = gate * sigmoid
    gate_delta = (back * up * sigmoid * (1.0 + gate * (1.0 - sigmoid))).astype(BF)
    up_delta = (back * silu).astype(BF)
    terms_ref[:, :ffw] = gate_delta
    terms_ref[:, ffw : 2 * ffw] = up_delta
    terms_ref[:, 2 * ffw :] = (silu * up).astype(BF)
    for j in range(pieces, MAIN):
        packed[:, j, :] = jnp.zeros((m, LANES), F32)
    for q in range(groups):
        out = dot(gate_delta, weights_ref[q, :, :ffw], CONTRACT_LAST)
        out = out + dot(up_delta, weights_ref[q, :, ffw:], CONTRACT_LAST)
        out_back_ref[q, :, :quarter] = out[:n, :].astype(BF)
        for j in range(pieces):
            packed[:, j, :] = out[n:, j * LANES : (j + 1) * LANES]
        out_back_ref[q, :, quarter:] = packed[...].reshape(n, LANES).astype(BF)


def row_blocks(rows_ref, packed, quarter, which):
    sources = rows_ref.shape[0] // MAIN
    pieces = quarter // LANES
    packed[...] = (
        rows_ref[:, quarter : quarter + LANES].astype(F32).reshape(sources, MAIN, LANES)
    )
    n, m = rows_ref.shape[0] // 4, sources // 4
    first = which * (quarter + LANES)
    columns = slice(first, first + quarter)
    for r in range(4):
        extra = jnp.concatenate(
            [packed[r * m : (r + 1) * m, which * pieces + j, :] for j in range(pieces)], axis=1
        )
        yield r * (n + m), n, m, rows_ref[r * n : (r + 1) * n, columns], extra.astype(BF)


def token_weights_kernel(rows_ref, terms_ref, gate_ref, up_ref, packed):
    quarter, ffw = gate_ref.shape
    total = 0.0
    for at, n, m, rows, extra in row_blocks(rows_ref, packed, quarter, 0):
        total = total + dot(rows, terms_ref[at : at + n, : 2 * ffw], CONTRACT_FIRST)
        total = total + dot(extra, terms_ref[at + n : at + n + m, : 2 * ffw], CONTRACT_FIRST)
    gate_ref[...] = total[:, :ffw].astype(BF)
    up_ref[...] = total[:, ffw:].astype(BF)


def down_weights_kernel(rows_ref, terms_ref, down_ref, packed):
    ffw, quarter = down_ref.shape
    total = 0.0
    for at, n, m, rows, extra in row_blocks(rows_ref, packed, quarter, 1):
        total = total + dot(terms_ref[at : at + n, 2 * ffw :], rows, CONTRACT_FIRST)
        total = total + dot(terms_ref[at + n : at + n + m, 2 * ffw :], extra, CONTRACT_FIRST)
    down_ref[...] = total.astype(BF)


def combine_kernel(ids_ref, rows_ref, out_ref, packed):
    experts = rows_ref.shape[0] // MAIN
    quarter = out_ref.shape[1]
    slot, _ = routing(ids_ref, experts)
    here = jnp.where(main_slots(slot), 1.0, 0.0).astype(BF)
    last = jnp.where(slot == float(MAIN), 1.0, 0.0).astype(BF)
    packed[...] = rows_ref[:, quarter:].astype(F32).reshape(experts, MAIN, LANES)
    total = dot(here, rows_ref[:, :quarter], CONTRACT_FIRST)
    for j in range(quarter // LANES):
        at = slice(j * LANES, (j + 1) * LANES)
        extra = dot(last, packed[:, j, :].astype(BF), CONTRACT_FIRST)
        out_ref[:, at] = (total[:, at] + extra).astype(BF)


def exchange(blocks, axis):
    return lax.all_to_all(blocks, axis, split_axis=0, concat_axis=0, tiled=True)


def body(tokens, out_grad, expert_ids, route_weight, w_gate, w_up, w_down):
    experts = lax.axis_size("ep")
    groups = lax.axis_size("rep")
    count, quarter = tokens.shape
    ffw = w_gate.shape[2]
    main = experts * MAIN
    n, m = main // groups, experts // groups
    shape = jax.ShapeDtypeStruct
    packed = pltpu.VMEM((experts, MAIN, LANES), F32)

    weights = kernel_call(
        pack_weights_kernel,
        shape((quarter, 2 * ffw), BF),
        (w_gate[0], w_up[0]),
        0,
        vmem=60,
    )
    weights = lax.all_gather(weights, "rep", axis=0)
    ids = expert_ids.T
    sent = kernel_call(
        dispatch_kernel,
        shape((main, 2 * quarter + LANES), BF),
        (ids, route_weight.T, tokens, out_grad),
        4 * main * count * quarter,
        (
            packed,
            pltpu.VMEM((count, quarter), BF),
            pltpu.VMEM((count, quarter), BF),
            pltpu.SemaphoreType.DMA((2,)),
        ),
        in_hbm=(2, 3),
    )
    rows = exchange(sent.reshape(experts, MAIN, -1), "ep").reshape(main, -1)
    back_parts = kernel_call(
        grad_products_kernel,
        shape((main + experts, ffw), BF),
        (rows, w_down[0]),
        2 * (main + experts) * quarter * ffw,
        (packed,),
    )
    token_rows, back_parts, weights = lax.optimization_barrier(
        (rows[:, : quarter + LANES], back_parts, weights)
    )
    back_sums = lax.psum_scatter(back_parts, "rep", scatter_dimension=0, tiled=True)
    wide_rows = exchange(token_rows.reshape(groups, n, -1), "rep")
    terms, back = kernel_call(
        expert_kernel,
        (shape((n + m, 3 * ffw), BF), shape((groups, n, quarter + LANES), BF)),
        (wide_rows, weights, back_sums),
        8 * (n + m) * groups * quarter * ffw,
        (
            pltpu.VMEM((groups, n, quarter + LANES), BF),
            pltpu.VMEM((groups, quarter, 2 * ffw), BF),
            pltpu.VMEM((n + m, ffw), BF),
            pltpu.VMEM((m, MAIN, LANES), F32),
            pltpu.SemaphoreType.DMA((2, groups + 1)),
        ),
        in_hbm=(0, 1, 2),
        vmem=60,
    )
    terms = lax.all_gather(terms, "rep", axis=0, tiled=True)
    back = exchange(back, "rep")
    returned = exchange(back.reshape(experts, MAIN, -1), "ep").reshape(main, -1)
    grad_gate, grad_up = kernel_call(
        token_weights_kernel,
        (shape((quarter, ffw), BF), shape((quarter, ffw), BF)),
        (rows, terms),
        4 * (main + experts) * quarter * ffw,
        (packed,),
    )
    grad_down = kernel_call(
        down_weights_kernel,
        shape((ffw, quarter), BF),
        (rows, terms),
        2 * (main + experts) * quarter * ffw,
        (packed,),
    )
    ids, grad_gate, grad_up, grad_down = lax.optimization_barrier(
        (ids, grad_gate, grad_up, grad_down)
    )
    token_grad = kernel_call(
        combine_kernel,
        shape((count, quarter), BF),
        (ids, returned),
        2 * main * count * quarter,
        (packed,),
    )
    return token_grad, grad_gate[None], grad_up[None], grad_down[None]


def solution(mesh):
    rows = P("ep", "rep")
    by_width = P("ep", "rep", None)
    last = P("ep", None, "rep")
    return jax.shard_map(
        body,
        mesh=mesh,
        in_specs=(rows, rows, P("ep", None), P("ep", None), by_width, by_width, last),
        out_specs=(rows, by_width, by_width, last),
        check_vma=False,
    )
```

```python
import jax
import jax.numpy as jnp
from jax import lax
from jax.experimental import pallas as pl
from jax.experimental.pallas import tpu as pltpu
from jax.sharding import PartitionSpec as P

MAIN = 8
LANES = 128
BF = jnp.bfloat16
F32 = jnp.float32
CONTRACT_LAST = (((1,), (1,)), ((), ()))
CONTRACT_FIRST = (((0,), (0,)), ((), ()))


def dot(a, b, dims=(((1,), (0,)), ((), ()))):
    return lax.dot_general(a, b, dims, preferred_element_type=F32)


def kernel_call(body, out_shape, args, flops, scratch=(), in_hbm=(), vmem=48):
    moved = sum(a.size * a.dtype.itemsize for a in args)
    outs = out_shape if isinstance(out_shape, tuple) else (out_shape,)
    moved += sum(o.size * o.dtype.itemsize for o in outs)
    return pl.pallas_call(
        body,
        out_shape=out_shape,
        in_specs=[
            pl.BlockSpec(memory_space=pl.ANY if i in in_hbm else pltpu.VMEM)
            for i in range(len(args))
        ],
        out_specs=jax.tree.map(lambda _: pl.BlockSpec(memory_space=pltpu.VMEM), out_shape),
        scratch_shapes=list(scratch),
        compiler_params=pltpu.CompilerParams(vmem_limit_bytes=vmem << 20),
        cost_estimate=pl.CostEstimate(flops=flops, bytes_accessed=moved, transcendentals=0),
    )(*args)


def routing(ids_ref, experts):
    top, count = ids_ref.shape
    expert = lax.broadcasted_iota(jnp.int32, (experts, count), 0)
    matches = [expert == ids_ref[k : k + 1, :] for k in range(top)]
    picked = sum(m.astype(F32) for m in matches)
    earlier = lax.broadcasted_iota(jnp.int32, (count, count), 0) < lax.broadcasted_iota(
        jnp.int32, (count, count), 1
    )
    before = dot(picked.astype(BF), earlier.astype(F32).astype(BF))
    return jnp.where(picked > 0.0, before, -1.0), matches


def spread(per_expert):
    experts, count = per_expert.shape
    wide = jnp.broadcast_to(per_expert[:, None, :], (experts, MAIN, count))
    return wide.reshape(experts * MAIN, count)


def main_slots(slot):
    experts, count = slot.shape
    number = lax.broadcasted_iota(jnp.int32, (experts * MAIN, count), 0) % MAIN
    return spread(slot) == number.astype(F32)


def pack_weights_kernel(gate_ref, up_ref, out_ref):
    ffw = gate_ref.shape[1]
    out_ref[:, :ffw] = gate_ref[...]
    out_ref[:, ffw:] = up_ref[...]


def dispatch_kernel(
    ids_ref, weight_ref, tokens_hbm, grads_hbm, out_ref, packed, tokens_ref, grads_ref, sems
):
    loads = (
        pltpu.make_async_copy(tokens_hbm, tokens_ref, sems.at[0]),
        pltpu.make_async_copy(grads_hbm, grads_ref, sems.at[1]),
    )
    for load in loads:
        load.start()
    experts = out_ref.shape[0] // MAIN
    quarter = tokens_ref.shape[1]
    slot, matches = routing(ids_ref, experts)
    weight = sum(
        jnp.where(m, weight_ref[k : k + 1, :].astype(F32), 0.0) for k, m in enumerate(matches)
    )
    here = main_slots(slot)
    placing = jnp.where(here, 1.0, 0.0).astype(BF)
    weighing = jnp.where(here, spread(weight), 0.0).astype(BF)
    loads[0].wait()
    out_ref[:, :quarter] = dot(placing, tokens_ref[...]).astype(BF)
    loads[1].wait()
    out_ref[:, quarter + LANES :] = dot(weighing, grads_ref[...]).astype(BF)
    last = slot == float(MAIN)
    extra_tokens = dot(jnp.where(last, 1.0, 0.0).astype(BF), tokens_ref[...])
    extra_grads = dot(jnp.where(last, weight, 0.0).astype(BF), grads_ref[...])
    pieces = quarter // LANES
    for j in range(pieces):
        packed[:, j, :] = extra_tokens[:, j * LANES : (j + 1) * LANES]
        packed[:, pieces + j, :] = extra_grads[:, j * LANES : (j + 1) * LANES]
    out_ref[:, quarter : quarter + LANES] = (
        packed[...].reshape(experts * MAIN, LANES).astype(BF)
    )


def grad_products_kernel(rows_ref, down_ref, out_ref, packed):
    quarter = down_ref.shape[1]
    for at, n, m, rows, extra in row_blocks(rows_ref, packed, quarter, 1):
        out_ref[at : at + n, :] = dot(rows, down_ref[...], CONTRACT_LAST).astype(BF)
        out_ref[at + n : at + n + m, :] = dot(extra, down_ref[...], CONTRACT_LAST).astype(BF)


def token_products_kernel(
    rows_hbm, weights_hbm, gate_ref, up_ref, rows_ref, weights_ref, packed, sems
):
    groups, n, _ = rows_ref.shape
    quarter = weights_ref.shape[1]
    ffw = weights_ref.shape[2] // 2
    m = n // MAIN
    pieces = quarter // LANES
    loads = []
    for q in range(groups):
        load = (
            pltpu.make_async_copy(rows_hbm.at[q], rows_ref.at[q], sems.at[0, q]),
            pltpu.make_async_copy(weights_hbm.at[q], weights_ref.at[q], sems.at[1, q]),
        )
        load[0].start()
        load[1].start()
        loads.append(load)
    gate, up = 0.0, 0.0
    for q, (rows, weights) in enumerate(loads):
        rows.wait()
        packed[...] = rows_ref[q, :, quarter:].astype(F32).reshape(m, MAIN, LANES)
        extra = [packed[:, j, :].astype(BF) for j in range(pieces)]
        token_rows = jnp.concatenate(
            [rows_ref[q, :, :quarter], jnp.concatenate(extra, axis=1)], axis=0
        )
        weights.wait()
        gate = gate + dot(token_rows, weights_ref[q, :, :ffw])
        up = up + dot(token_rows, weights_ref[q, :, ffw:])
    gate_ref[...] = gate
    up_ref[...] = up


def expert_kernel(
    weights_hbm, gate_hbm, up_hbm, back_hbm, terms_ref, out_back_ref, *scratch
):
    weights_ref, gate_ref, up_ref, back_ref, packed, sems = scratch
    groups, n, _ = out_back_ref.shape
    quarter = weights_ref.shape[1]
    ffw = weights_ref.shape[2] // 2
    m = n // MAIN
    pieces = quarter // LANES
    small = [
        pltpu.make_async_copy(src, dst, sems.at[1, i])
        for i, (src, dst) in enumerate(
            ((gate_hbm, gate_ref), (up_hbm, up_ref), (back_hbm, back_ref))
        )
    ]
    loads = [
        pltpu.make_async_copy(weights_hbm.at[q], weights_ref.at[q], sems.at[0, q])
        for q in range(groups)
    ]
    for load in small + loads:
        load.start()
    for load in small:
        load.wait()
    gate, up, back = gate_ref[...], up_ref[...], back_ref[...].astype(F32)
    sigmoid = 1.0 / (1.0 + jnp.exp(-gate))
    silu = gate * sigmoid
    gate_delta = (back * up * sigmoid * (1.0 + gate * (1.0 - sigmoid))).astype(BF)
    up_delta = (back * silu).astype(BF)
    terms_ref[:, :ffw] = gate_delta
    terms_ref[:, ffw : 2 * ffw] = up_delta
    terms_ref[:, 2 * ffw :] = (silu * up).astype(BF)
    for j in range(pieces, MAIN):
        packed[:, j, :] = jnp.zeros((m, LANES), F32)
    for q in range(groups):
        loads[q].wait()
        out = dot(gate_delta, weights_ref[q, :, :ffw], CONTRACT_LAST)
        out = out + dot(up_delta, weights_ref[q, :, ffw:], CONTRACT_LAST)
        out_back_ref[q, :, :quarter] = out[:n, :].astype(BF)
        for j in range(pieces):
            packed[:, j, :] = out[n:, j * LANES : (j + 1) * LANES]
        out_back_ref[q, :, quarter:] = packed[...].reshape(n, LANES).astype(BF)


def row_blocks(rows_ref, packed, quarter, which):
    sources = rows_ref.shape[0] // MAIN
    pieces = quarter // LANES
    packed[...] = (
        rows_ref[:, quarter : quarter + LANES].astype(F32).reshape(sources, MAIN, LANES)
    )
    n, m = rows_ref.shape[0] // 4, sources // 4
    first = which * (quarter + LANES)
    columns = slice(first, first + quarter)
    for r in range(4):
        extra = jnp.concatenate(
            [packed[r * m : (r + 1) * m, which * pieces + j, :] for j in range(pieces)], axis=1
        )
        yield r * (n + m), n, m, rows_ref[r * n : (r + 1) * n, columns], extra.astype(BF)


def token_weights_kernel(rows_ref, terms_ref, gate_ref, up_ref, packed):
    quarter, ffw = gate_ref.shape
    total = 0.0
    for at, n, m, rows, extra in row_blocks(rows_ref, packed, quarter, 0):
        total = total + dot(rows, terms_ref[at : at + n, : 2 * ffw], CONTRACT_FIRST)
        total = total + dot(extra, terms_ref[at + n : at + n + m, : 2 * ffw], CONTRACT_FIRST)
    gate_ref[...] = total[:, :ffw].astype(BF)
    up_ref[...] = total[:, ffw:].astype(BF)


def down_weights_kernel(rows_ref, terms_ref, down_ref, packed):
    ffw, quarter = down_ref.shape
    total = 0.0
    for at, n, m, rows, extra in row_blocks(rows_ref, packed, quarter, 1):
        total = total + dot(terms_ref[at : at + n, 2 * ffw :], rows, CONTRACT_FIRST)
        total = total + dot(terms_ref[at + n : at + n + m, 2 * ffw :], extra, CONTRACT_FIRST)
    down_ref[...] = total.astype(BF)


def combine_kernel(ids_ref, rows_hbm, out_ref, packed, rows_ref, sem):
    load = pltpu.make_async_copy(rows_hbm, rows_ref, sem)
    load.start()
    experts = rows_ref.shape[0] // MAIN
    quarter = out_ref.shape[1]
    slot, _ = routing(ids_ref, experts)
    here = jnp.where(main_slots(slot), 1.0, 0.0).astype(BF)
    last = jnp.where(slot == float(MAIN), 1.0, 0.0).astype(BF)
    load.wait()
    packed[...] = rows_ref[:, quarter:].astype(F32).reshape(experts, MAIN, LANES)
    total = dot(here, rows_ref[:, :quarter], CONTRACT_FIRST)
    for j in range(quarter // LANES):
        at = slice(j * LANES, (j + 1) * LANES)
        extra = dot(last, packed[:, j, :].astype(BF), CONTRACT_FIRST)
        out_ref[:, at] = (total[:, at] + extra).astype(BF)


def exchange(blocks, axis):
    return lax.all_to_all(blocks, axis, split_axis=0, concat_axis=0, tiled=True)


def body(tokens, out_grad, expert_ids, route_weight, w_gate, w_up, w_down):
    experts = lax.axis_size("ep")
    groups = lax.axis_size("rep")
    count, quarter = tokens.shape
    ffw = w_gate.shape[2]
    main = experts * MAIN
    n, m = main // groups, experts // groups
    shape = jax.ShapeDtypeStruct
    packed = pltpu.VMEM((experts, MAIN, LANES), F32)

    weights = kernel_call(
        pack_weights_kernel,
        shape((quarter, 2 * ffw), BF),
        (w_gate[0], w_up[0]),
        0,
        vmem=60,
    )
    weights = lax.all_gather(weights, "rep", axis=0)
    ids = expert_ids.T
    sent = kernel_call(
        dispatch_kernel,
        shape((main, 2 * quarter + LANES), BF),
        (ids, route_weight.T, tokens, out_grad),
        4 * main * count * quarter,
        (
            packed,
            pltpu.VMEM((count, quarter), BF),
            pltpu.VMEM((count, quarter), BF),
            pltpu.SemaphoreType.DMA((2,)),
        ),
        in_hbm=(2, 3),
    )
    rows = exchange(sent.reshape(experts, MAIN, -1), "ep").reshape(main, -1)
    back_parts = kernel_call(
        grad_products_kernel,
        shape((main + experts, ffw), BF),
        (rows, w_down[0]),
        2 * (main + experts) * quarter * ffw,
        (packed,),
    )
    token_rows, back_parts, weights = lax.optimization_barrier(
        (rows[:, : quarter + LANES], back_parts, weights)
    )
    back_sums = lax.psum_scatter(back_parts, "rep", scatter_dimension=0, tiled=True)
    wide_rows = exchange(token_rows.reshape(groups, n, -1), "rep")
    gate, up = kernel_call(
        token_products_kernel,
        (shape((n + m, ffw), F32), shape((n + m, ffw), F32)),
        (wide_rows, weights),
        4 * (n + m) * groups * quarter * ffw,
        (
            pltpu.VMEM((groups, n, quarter + LANES), BF),
            pltpu.VMEM((groups, quarter, 2 * ffw), BF),
            pltpu.VMEM((m, MAIN, LANES), F32),
            pltpu.SemaphoreType.DMA((2, groups)),
        ),
        in_hbm=(0, 1),
        vmem=60,
    )
    terms, back = kernel_call(
        expert_kernel,
        (shape((n + m, 3 * ffw), BF), shape((groups, n, quarter + LANES), BF)),
        (weights, gate, up, back_sums),
        4 * (n + m) * groups * quarter * ffw,
        (
            pltpu.VMEM((groups, quarter, 2 * ffw), BF),
            pltpu.VMEM((n + m, ffw), F32),
            pltpu.VMEM((n + m, ffw), F32),
            pltpu.VMEM((n + m, ffw), BF),
            pltpu.VMEM((m, MAIN, LANES), F32),
            pltpu.SemaphoreType.DMA((2, groups)),
        ),
        in_hbm=(0, 1, 2, 3),
        vmem=60,
    )
    terms = lax.all_gather(terms, "rep", axis=0, tiled=True)
    back = exchange(back, "rep")
    returned = exchange(back.reshape(experts, MAIN, -1), "ep").reshape(main, -1)
    grad_gate, grad_up = kernel_call(
        token_weights_kernel,
        (shape((quarter, ffw), BF), shape((quarter, ffw), BF)),
        (rows, terms),
        4 * (main + experts) * quarter * ffw,
        (packed,),
    )
    grad_down = kernel_call(
        down_weights_kernel,
        shape((ffw, quarter), BF),
        (rows, terms),
        2 * (main + experts) * quarter * ffw,
        (packed,),
    )
    ids, grad_gate, grad_up, grad_down = lax.optimization_barrier(
        (ids, grad_gate, grad_up, grad_down)
    )
    token_grad = kernel_call(
        combine_kernel,
        shape((count, quarter), BF),
        (ids, returned),
        2 * main * count * quarter,
        (packed, pltpu.VMEM((main, quarter + LANES), BF), pltpu.SemaphoreType.DMA),
        in_hbm=(1,),
        vmem=60,
    )
    return token_grad, grad_gate[None], grad_up[None], grad_down[None]


def solution(mesh):
    rows = P("ep", "rep")
    by_width = P("ep", "rep", None)
    last = P("ep", None, "rep")
    return jax.shard_map(
        body,
        mesh=mesh,
        in_specs=(rows, rows, P("ep", None), P("ep", None), by_width, by_width, last),
        out_specs=(rows, by_width, by_width, last),
        check_vma=False,
    )
```

```python
import jax
import jax.numpy as jnp
from jax import lax
from jax.experimental import pallas as pl
from jax.experimental.pallas import tpu as pltpu
from jax.sharding import PartitionSpec as P

MAIN = 8
LANES = 128
BF = jnp.bfloat16
F32 = jnp.float32
CONTRACT_LAST = (((1,), (1,)), ((), ()))
CONTRACT_FIRST = (((0,), (0,)), ((), ()))


def dot(a, b, dims=(((1,), (0,)), ((), ()))):
    return lax.dot_general(a, b, dims, preferred_element_type=F32)


def kernel_call(body, out_shape, args, flops, scratch=(), in_hbm=(), in_smem=(), vmem=48):
    moved = sum(a.size * a.dtype.itemsize for a in args)
    outs = out_shape if isinstance(out_shape, tuple) else (out_shape,)
    moved += sum(o.size * o.dtype.itemsize for o in outs)
    return pl.pallas_call(
        body,
        out_shape=out_shape,
        in_specs=[
            pl.BlockSpec(
                memory_space=pl.ANY if i in in_hbm else pltpu.SMEM if i in in_smem else pltpu.VMEM
            )
            for i in range(len(args))
        ],
        out_specs=jax.tree.map(lambda _: pl.BlockSpec(memory_space=pltpu.VMEM), out_shape),
        scratch_shapes=list(scratch),
        compiler_params=pltpu.CompilerParams(vmem_limit_bytes=vmem << 20),
        cost_estimate=pl.CostEstimate(flops=flops, bytes_accessed=moved, transcendentals=0),
    )(*args)


def routing(ids_ref, experts):
    top, count = ids_ref.shape
    expert = lax.broadcasted_iota(jnp.int32, (experts, count), 0)
    matches = [expert == ids_ref[k : k + 1, :] for k in range(top)]
    picked = sum(m.astype(F32) for m in matches)
    earlier = lax.broadcasted_iota(jnp.int32, (count, count), 0) < lax.broadcasted_iota(
        jnp.int32, (count, count), 1
    )
    before = dot(picked.astype(BF), earlier.astype(F32).astype(BF))
    return jnp.where(picked > 0.0, before, -1.0), matches


def spread(per_expert):
    experts, count = per_expert.shape
    wide = jnp.broadcast_to(per_expert[:, None, :], (experts, MAIN, count))
    return wide.reshape(experts * MAIN, count)


def main_slots(slot):
    experts, count = slot.shape
    number = lax.broadcasted_iota(jnp.int32, (experts * MAIN, count), 0) % MAIN
    return spread(slot) == number.astype(F32)


def pack_weights_kernel(gate_ref, up_ref, out_ref):
    ffw = gate_ref.shape[1]
    out_ref[:, :ffw] = gate_ref[...]
    out_ref[:, ffw:] = up_ref[...]


def dispatch_kernel(
    ids_ref, weight_ref, tokens_hbm, grads_hbm, out_ref, packed, tokens_ref, grads_ref, sems
):
    loads = (
        pltpu.make_async_copy(tokens_hbm, tokens_ref, sems.at[0]),
        pltpu.make_async_copy(grads_hbm, grads_ref, sems.at[1]),
    )
    for load in loads:
        load.start()
    experts = out_ref.shape[0] // MAIN
    quarter = tokens_ref.shape[1]
    slot, matches = routing(ids_ref, experts)
    weight = sum(
        jnp.where(m, weight_ref[k : k + 1, :].astype(F32), 0.0) for k, m in enumerate(matches)
    )
    here = main_slots(slot)
    placing = jnp.where(here, 1.0, 0.0).astype(BF)
    weighing = jnp.where(here, spread(weight), 0.0).astype(BF)
    loads[0].wait()
    out_ref[:, :quarter] = dot(placing, tokens_ref[...]).astype(BF)
    loads[1].wait()
    out_ref[:, quarter + LANES :] = dot(weighing, grads_ref[...]).astype(BF)
    last = slot == float(MAIN)
    extra_tokens = dot(jnp.where(last, 1.0, 0.0).astype(BF), tokens_ref[...])
    extra_grads = dot(jnp.where(last, weight, 0.0).astype(BF), grads_ref[...])
    pieces = quarter // LANES
    for j in range(pieces):
        packed[:, j, :] = extra_tokens[:, j * LANES : (j + 1) * LANES]
        packed[:, pieces + j, :] = extra_grads[:, j * LANES : (j + 1) * LANES]
    out_ref[:, quarter : quarter + LANES] = (
        packed[...].reshape(experts * MAIN, LANES).astype(BF)
    )


def grad_products_kernel(rank_ref, rows_ref, down_ref, out_ref, *refs):
    *token_refs, packed = refs
    quarter = down_ref.shape[1]
    groups, count = len(token_refs), token_refs[0].shape[0]
    for k, token_ref in enumerate(token_refs):
        first = pl.multiple_of(away(rank_ref, k, groups) * count, count)
        token_ref[...] = rows_ref[pl.ds(first, count), : quarter + LANES]
    for at, n, m, rows, extra in row_blocks(rows_ref, packed, quarter, 1):
        out_ref[at : at + n, :] = dot(rows, down_ref[...], CONTRACT_LAST).astype(BF)
        out_ref[at + n : at + n + m, :] = dot(extra, down_ref[...], CONTRACT_LAST).astype(BF)


def away(rank_ref, k, groups):
    return lax.rem(rank_ref[0] + (k + groups), groups)


def token_products_kernel(rank_ref, weights_hbm, *refs):
    *rows_hbm, gate_ref, up_ref, rows_ref, weights_ref, packed, sems = refs
    groups, n, _ = rows_ref.shape
    quarter = weights_ref.shape[1]
    ffw = weights_ref.shape[2] // 2
    m = n // MAIN
    pieces = quarter // LANES
    loads = []
    for q in range(groups):
        load = (
            pltpu.make_async_copy(rows_hbm[q], rows_ref.at[q], sems.at[0, q]),
            pltpu.make_async_copy(
                weights_hbm.at[away(rank_ref, -q, groups)], weights_ref.at[q], sems.at[1, q]
            ),
        )
        load[0].start()
        load[1].start()
        loads.append(load)
    gate, up = 0.0, 0.0
    for q, (rows, weights) in enumerate(loads):
        rows.wait()
        packed[...] = rows_ref[q, :, quarter:].astype(F32).reshape(m, MAIN, LANES)
        extra = [packed[:, j, :].astype(BF) for j in range(pieces)]
        token_rows = jnp.concatenate(
            [rows_ref[q, :, :quarter], jnp.concatenate(extra, axis=1)], axis=0
        )
        weights.wait()
        gate = gate + dot(token_rows, weights_ref[q, :, :ffw])
        up = up + dot(token_rows, weights_ref[q, :, ffw:])
    gate_ref[...] = gate
    up_ref[...] = up


def place_kernel(rank_ref, *refs):
    *blocks, out_ref = refs
    for k, block in enumerate(blocks):
        out_ref[away(rank_ref, -k, len(blocks))] = block[...]


def expert_kernel(rank_ref, weights_hbm, gate_hbm, up_hbm, back_hbm, terms_ref, *refs):
    *out_back_refs, weights_ref, gate_ref, up_ref, back_ref, packed, sems = refs
    groups, n = len(out_back_refs), out_back_refs[0].shape[0]
    quarter = weights_ref.shape[1]
    ffw = weights_ref.shape[2] // 2
    m = n // MAIN
    pieces = quarter // LANES
    small = [
        pltpu.make_async_copy(src, dst, sems.at[1, i])
        for i, (src, dst) in enumerate(
            ((gate_hbm, gate_ref), (up_hbm, up_ref), (back_hbm, back_ref))
        )
    ]
    loads = [
        pltpu.make_async_copy(
            weights_hbm.at[away(rank_ref, q, groups)], weights_ref.at[q], sems.at[0, q]
        )
        for q in range(groups)
    ]
    for load in small + loads:
        load.start()
    for load in small:
        load.wait()
    gate, up, back = gate_ref[...], up_ref[...], back_ref[...].astype(F32)
    sigmoid = 1.0 / (1.0 + jnp.exp(-gate))
    silu = gate * sigmoid
    gate_delta = (back * up * sigmoid * (1.0 + gate * (1.0 - sigmoid))).astype(BF)
    up_delta = (back * silu).astype(BF)
    terms_ref[:, :ffw] = gate_delta
    terms_ref[:, ffw : 2 * ffw] = up_delta
    terms_ref[:, 2 * ffw :] = (silu * up).astype(BF)
    for j in range(pieces, MAIN):
        packed[:, j, :] = jnp.zeros((m, LANES), F32)
    for q in range(groups):
        loads[q].wait()
        out = dot(gate_delta, weights_ref[q, :, :ffw], CONTRACT_LAST)
        out = out + dot(up_delta, weights_ref[q, :, ffw:], CONTRACT_LAST)
        out_back_refs[q][:, :quarter] = out[:n, :].astype(BF)
        for j in range(pieces):
            packed[:, j, :] = out[n:, j * LANES : (j + 1) * LANES]
        out_back_refs[q][:, quarter:] = packed[...].reshape(n, LANES).astype(BF)


def row_blocks(rows_ref, packed, quarter, which):
    sources = rows_ref.shape[0] // MAIN
    pieces = quarter // LANES
    packed[...] = (
        rows_ref[:, quarter : quarter + LANES].astype(F32).reshape(sources, MAIN, LANES)
    )
    n, m = rows_ref.shape[0] // 4, sources // 4
    first = which * (quarter + LANES)
    columns = slice(first, first + quarter)
    for r in range(4):
        extra = jnp.concatenate(
            [packed[r * m : (r + 1) * m, which * pieces + j, :] for j in range(pieces)], axis=1
        )
        yield r * (n + m), n, m, rows_ref[r * n : (r + 1) * n, columns], extra.astype(BF)


def token_weights_kernel(rows_ref, terms_ref, gate_ref, up_ref, packed):
    quarter, ffw = gate_ref.shape
    total = 0.0
    for at, n, m, rows, extra in row_blocks(rows_ref, packed, quarter, 0):
        total = total + dot(rows, terms_ref[at : at + n, : 2 * ffw], CONTRACT_FIRST)
        total = total + dot(extra, terms_ref[at + n : at + n + m, : 2 * ffw], CONTRACT_FIRST)
    gate_ref[...] = total[:, :ffw].astype(BF)
    up_ref[...] = total[:, ffw:].astype(BF)


def down_weights_kernel(rows_ref, terms_ref, down_ref, packed):
    ffw, quarter = down_ref.shape
    total = 0.0
    for at, n, m, rows, extra in row_blocks(rows_ref, packed, quarter, 1):
        total = total + dot(terms_ref[at : at + n, 2 * ffw :], rows, CONTRACT_FIRST)
        total = total + dot(terms_ref[at + n : at + n + m, 2 * ffw :], extra, CONTRACT_FIRST)
    down_ref[...] = total.astype(BF)


def combine_kernel(ids_ref, rows_ref, out_ref, packed):
    experts = rows_ref.shape[0] // MAIN
    quarter = out_ref.shape[1]
    slot, _ = routing(ids_ref, experts)
    here = jnp.where(main_slots(slot), 1.0, 0.0).astype(BF)
    last = jnp.where(slot == float(MAIN), 1.0, 0.0).astype(BF)
    packed[...] = rows_ref[:, quarter:].astype(F32).reshape(experts, MAIN, LANES)
    total = dot(here, rows_ref[:, :quarter], CONTRACT_FIRST)
    for j in range(quarter // LANES):
        at = slice(j * LANES, (j + 1) * LANES)
        extra = dot(last, packed[:, j, :].astype(BF), CONTRACT_FIRST)
        out_ref[:, at] = (total[:, at] + extra).astype(BF)


def exchange(blocks, axis):
    return lax.all_to_all(blocks, axis, split_axis=0, concat_axis=0, tiled=True)


def swap(blocks, axis):
    groups = len(blocks)
    return blocks[:1] + [
        lax.ppermute(blocks[k], axis, [(i, (i + k) % groups) for i in range(groups)])
        for k in range(1, groups)
    ]


def body(tokens, out_grad, expert_ids, route_weight, w_gate, w_up, w_down):
    experts = lax.axis_size("ep")
    groups = lax.axis_size("rep")
    count, quarter = tokens.shape
    ffw = w_gate.shape[2]
    main = experts * MAIN
    n, m = main // groups, experts // groups
    shape = jax.ShapeDtypeStruct
    packed = pltpu.VMEM((experts, MAIN, LANES), F32)

    weights = kernel_call(
        pack_weights_kernel,
        shape((quarter, 2 * ffw), BF),
        (w_gate[0], w_up[0]),
        0,
        vmem=60,
    )
    weights = lax.all_gather(weights, "rep", axis=0)
    at_rank = lax.axis_index("rep").astype(jnp.int32).reshape(1)
    ids, at_rank = lax.optimization_barrier((expert_ids.T, at_rank))
    sent = kernel_call(
        dispatch_kernel,
        shape((main, 2 * quarter + LANES), BF),
        (ids, route_weight.T, tokens, out_grad),
        4 * main * count * quarter,
        (
            packed,
            pltpu.VMEM((count, quarter), BF),
            pltpu.VMEM((count, quarter), BF),
            pltpu.SemaphoreType.DMA((2,)),
        ),
        in_hbm=(2, 3),
    )
    rows = exchange(sent.reshape(experts, MAIN, -1), "ep").reshape(main, -1)
    back_parts, *token_rows = kernel_call(
        grad_products_kernel,
        (shape((main + experts, ffw), BF),) + (shape((n, quarter + LANES), BF),) * groups,
        (at_rank, rows, w_down[0]),
        2 * (main + experts) * quarter * ffw,
        (packed,),
        in_smem=(0,),
    )
    back_parts, weights = lax.optimization_barrier((back_parts, weights))
    back_sums = lax.psum_scatter(back_parts, "rep", scatter_dimension=0, tiled=True)
    wide_rows = swap(token_rows, "rep")
    gate, up = kernel_call(
        token_products_kernel,
        (shape((n + m, ffw), F32), shape((n + m, ffw), F32)),
        (at_rank, weights, *wide_rows),
        4 * (n + m) * groups * quarter * ffw,
        (
            pltpu.VMEM((groups, n, quarter + LANES), BF),
            pltpu.VMEM((groups, quarter, 2 * ffw), BF),
            pltpu.VMEM((m, MAIN, LANES), F32),
            pltpu.SemaphoreType.DMA((2, groups)),
        ),
        in_smem=(0,),
        in_hbm=range(1, 2 + groups),
        vmem=60,
    )
    terms, *back = kernel_call(
        expert_kernel,
        (shape((n + m, 3 * ffw), BF),) + (shape((n, quarter + LANES), BF),) * groups,
        (at_rank, weights, gate, up, back_sums),
        4 * (n + m) * groups * quarter * ffw,
        (
            pltpu.VMEM((groups, quarter, 2 * ffw), BF),
            pltpu.VMEM((n + m, ffw), F32),
            pltpu.VMEM((n + m, ffw), F32),
            pltpu.VMEM((n + m, ffw), BF),
            pltpu.VMEM((m, MAIN, LANES), F32),
            pltpu.SemaphoreType.DMA((2, groups)),
        ),
        in_smem=(0,),
        in_hbm=(1, 2, 3, 4),
        vmem=60,
    )
    terms = lax.all_gather(terms, "rep", axis=0, tiled=True)
    back = kernel_call(
        place_kernel,
        shape((groups, n, quarter + LANES), BF),
        (at_rank, *swap(back, "rep")),
        0,
        in_smem=(0,),
    )
    returned = exchange(back.reshape(experts, MAIN, -1), "ep").reshape(main, -1)
    grad_gate, grad_up = kernel_call(
        token_weights_kernel,
        (shape((quarter, ffw), BF), shape((quarter, ffw), BF)),
        (rows, terms),
        4 * (main + experts) * quarter * ffw,
        (packed,),
    )
    grad_down = kernel_call(
        down_weights_kernel,
        shape((ffw, quarter), BF),
        (rows, terms),
        2 * (main + experts) * quarter * ffw,
        (packed,),
    )
    ids, grad_gate, grad_up, grad_down = lax.optimization_barrier(
        (ids, grad_gate, grad_up, grad_down)
    )
    token_grad = kernel_call(
        combine_kernel,
        shape((count, quarter), BF),
        (ids, returned),
        2 * main * count * quarter,
        (packed,),
    )
    return token_grad, grad_gate[None], grad_up[None], grad_down[None]


def solution(mesh):
    rows = P("ep", "rep")
    by_width = P("ep", "rep", None)
    last = P("ep", None, "rep")
    return jax.shard_map(
        body,
        mesh=mesh,
        in_specs=(rows, rows, P("ep", None), P("ep", None), by_width, by_width, last),
        out_specs=(rows, by_width, by_width, last),
        check_vma=False,
    )
```

```python
import jax
import jax.numpy as jnp
from jax import lax
from jax.experimental import pallas as pl
from jax.experimental.pallas import tpu as pltpu
from jax.sharding import PartitionSpec as P

MAIN = 8
LANES = 128
BF = jnp.bfloat16
F32 = jnp.float32
CONTRACT_LAST = (((1,), (1,)), ((), ()))
CONTRACT_FIRST = (((0,), (0,)), ((), ()))


def dot(a, b, dims=(((1,), (0,)), ((), ()))):
    return lax.dot_general(a, b, dims, preferred_element_type=F32)


def kernel_call(body, out_shape, args, flops, scratch=(), in_hbm=(), vmem=48):
    moved = sum(a.size * a.dtype.itemsize for a in args)
    outs = out_shape if isinstance(out_shape, tuple) else (out_shape,)
    moved += sum(o.size * o.dtype.itemsize for o in outs)
    return pl.pallas_call(
        body,
        out_shape=out_shape,
        in_specs=[
            pl.BlockSpec(memory_space=pl.ANY if i in in_hbm else pltpu.VMEM)
            for i in range(len(args))
        ],
        out_specs=jax.tree.map(lambda _: pl.BlockSpec(memory_space=pltpu.VMEM), out_shape),
        scratch_shapes=list(scratch),
        compiler_params=pltpu.CompilerParams(vmem_limit_bytes=vmem << 20),
        cost_estimate=pl.CostEstimate(flops=flops, bytes_accessed=moved, transcendentals=0),
    )(*args)


def routing(ids_ref, experts):
    top, count = ids_ref.shape
    expert = lax.broadcasted_iota(jnp.int32, (experts, count), 0)
    matches = [expert == ids_ref[k : k + 1, :] for k in range(top)]
    picked = sum(m.astype(F32) for m in matches)
    earlier = lax.broadcasted_iota(jnp.int32, (count, count), 0) < lax.broadcasted_iota(
        jnp.int32, (count, count), 1
    )
    before = dot(picked.astype(BF), earlier.astype(F32).astype(BF))
    return jnp.where(picked > 0.0, before, -1.0), matches


def spread(per_expert):
    experts, count = per_expert.shape
    wide = jnp.broadcast_to(per_expert[:, None, :], (experts, MAIN, count))
    return wide.reshape(experts * MAIN, count)


def main_slots(slot):
    experts, count = slot.shape
    number = lax.broadcasted_iota(jnp.int32, (experts * MAIN, count), 0) % MAIN
    return spread(slot) == number.astype(F32)


def pack_weights_kernel(gate_ref, up_ref, out_ref):
    ffw = gate_ref.shape[1]
    out_ref[:, :ffw] = gate_ref[...]
    out_ref[:, ffw:] = up_ref[...]


def dispatch_kernel(
    ids_ref, weight_ref, tokens_hbm, grads_hbm, out_ref, packed, tokens_ref, grads_ref, sems
):
    loads = (
        pltpu.make_async_copy(tokens_hbm, tokens_ref, sems.at[0]),
        pltpu.make_async_copy(grads_hbm, grads_ref, sems.at[1]),
    )
    for load in loads:
        load.start()
    experts = out_ref.shape[0] // MAIN
    quarter = tokens_ref.shape[1]
    slot, matches = routing(ids_ref, experts)
    weight = sum(
        jnp.where(m, weight_ref[k : k + 1, :].astype(F32), 0.0) for k, m in enumerate(matches)
    )
    here = main_slots(slot)
    placing = jnp.where(here, 1.0, 0.0).astype(BF)
    weighing = jnp.where(here, spread(weight), 0.0).astype(BF)
    loads[0].wait()
    out_ref[:, :quarter] = dot(placing, tokens_ref[...]).astype(BF)
    loads[1].wait()
    out_ref[:, quarter + LANES :] = dot(weighing, grads_ref[...]).astype(BF)
    last = slot == float(MAIN)
    extra_tokens = dot(jnp.where(last, 1.0, 0.0).astype(BF), tokens_ref[...])
    extra_grads = dot(jnp.where(last, weight, 0.0).astype(BF), grads_ref[...])
    pieces = quarter // LANES
    for j in range(pieces):
        packed[:, j, :] = extra_tokens[:, j * LANES : (j + 1) * LANES]
        packed[:, pieces + j, :] = extra_grads[:, j * LANES : (j + 1) * LANES]
    out_ref[:, quarter : quarter + LANES] = (
        packed[...].reshape(experts * MAIN, LANES).astype(BF)
    )


def grad_products_kernel(rows_ref, down_ref, out_ref, token_ref, packed):
    quarter = down_ref.shape[1]
    token_ref[...] = rows_ref[:, : quarter + LANES]
    for at, n, m, rows, extra in row_blocks(rows_ref, packed, quarter, 1):
        out_ref[at : at + n, :] = dot(rows, down_ref[...], CONTRACT_LAST).astype(BF)
        out_ref[at + n : at + n + m, :] = dot(extra, down_ref[...], CONTRACT_LAST).astype(BF)


def expert_kernel(
    rows_hbm, weights_hbm, back_hbm, terms_ref, out_back_ref, rows_ref, weights_ref, back_ref, packed, sems
):
    groups, n, _ = rows_ref.shape
    quarter = weights_ref.shape[1]
    ffw = weights_ref.shape[2] // 2
    m = n // MAIN
    pieces = quarter // LANES
    loads = []
    for q in range(groups):
        load = (
            pltpu.make_async_copy(rows_hbm.at[q], rows_ref.at[q], sems.at[0, q]),
            pltpu.make_async_copy(weights_hbm.at[q], weights_ref.at[q], sems.at[1, q]),
        )
        load[0].start()
        load[1].start()
        loads.append(load)
    back_load = pltpu.make_async_copy(back_hbm, back_ref, sems.at[0, groups])
    back_load.start()

    gate, up = 0.0, 0.0
    for q, (rows, weights) in enumerate(loads):
        rows.wait()
        packed[...] = rows_ref[q, :, quarter:].astype(F32).reshape(m, MAIN, LANES)
        extra = [packed[:, j, :].astype(BF) for j in range(pieces)]
        token_rows = jnp.concatenate(
            [rows_ref[q, :, :quarter], jnp.concatenate(extra, axis=1)], axis=0
        )
        weights.wait()
        gate = gate + dot(token_rows, weights_ref[q, :, :ffw])
        up = up + dot(token_rows, weights_ref[q, :, ffw:])
    back_load.wait()
    back = back_ref[...].astype(F32)
    sigmoid = 1.0 / (1.0 + jnp.exp(-gate))
    silu = gate * sigmoid
    gate_delta = (back * up * sigmoid * (1.0 + gate * (1.0 - sigmoid))).astype(BF)
    up_delta = (back * silu).astype(BF)
    terms_ref[:, :ffw] = gate_delta
    terms_ref[:, ffw : 2 * ffw] = up_delta
    terms_ref[:, 2 * ffw :] = (silu * up).astype(BF)
    for j in range(pieces, MAIN):
        packed[:, j, :] = jnp.zeros((m, LANES), F32)
    for q in range(groups):
        out = dot(gate_delta, weights_ref[q, :, :ffw], CONTRACT_LAST)
        out = out + dot(up_delta, weights_ref[q, :, ffw:], CONTRACT_LAST)
        out_back_ref[q, :, :quarter] = out[:n, :].astype(BF)
        for j in range(pieces):
            packed[:, j, :] = out[n:, j * LANES : (j + 1) * LANES]
        out_back_ref[q, :, quarter:] = packed[...].reshape(n, LANES).astype(BF)


def row_blocks(rows_ref, packed, quarter, which):
    sources = rows_ref.shape[0] // MAIN
    pieces = quarter // LANES
    packed[...] = (
        rows_ref[:, quarter : quarter + LANES].astype(F32).reshape(sources, MAIN, LANES)
    )
    n, m = rows_ref.shape[0] // 4, sources // 4
    first = which * (quarter + LANES)
    columns = slice(first, first + quarter)
    for r in range(4):
        extra = jnp.concatenate(
            [packed[r * m : (r + 1) * m, which * pieces + j, :] for j in range(pieces)], axis=1
        )
        yield r * (n + m), n, m, rows_ref[r * n : (r + 1) * n, columns], extra.astype(BF)


def token_weights_kernel(rows_ref, terms_ref, gate_ref, up_ref, packed):
    quarter, ffw = gate_ref.shape
    total = 0.0
    for at, n, m, rows, extra in row_blocks(rows_ref, packed, quarter, 0):
        total = total + dot(rows, terms_ref[at : at + n, : 2 * ffw], CONTRACT_FIRST)
        total = total + dot(extra, terms_ref[at + n : at + n + m, : 2 * ffw], CONTRACT_FIRST)
    gate_ref[...] = total[:, :ffw].astype(BF)
    up_ref[...] = total[:, ffw:].astype(BF)


def down_weights_kernel(rows_ref, terms_ref, down_ref, packed):
    ffw, quarter = down_ref.shape
    total = 0.0
    for at, n, m, rows, extra in row_blocks(rows_ref, packed, quarter, 1):
        total = total + dot(terms_ref[at : at + n, 2 * ffw :], rows, CONTRACT_FIRST)
        total = total + dot(terms_ref[at + n : at + n + m, 2 * ffw :], extra, CONTRACT_FIRST)
    down_ref[...] = total.astype(BF)


def combine_kernel(ids_ref, rows_ref, out_ref, packed):
    experts = rows_ref.shape[0] // MAIN
    quarter = out_ref.shape[1]
    slot, _ = routing(ids_ref, experts)
    here = jnp.where(main_slots(slot), 1.0, 0.0).astype(BF)
    last = jnp.where(slot == float(MAIN), 1.0, 0.0).astype(BF)
    packed[...] = rows_ref[:, quarter:].astype(F32).reshape(experts, MAIN, LANES)
    total = dot(here, rows_ref[:, :quarter], CONTRACT_FIRST)
    for j in range(quarter // LANES):
        at = slice(j * LANES, (j + 1) * LANES)
        extra = dot(last, packed[:, j, :].astype(BF), CONTRACT_FIRST)
        out_ref[:, at] = (total[:, at] + extra).astype(BF)


def exchange(blocks, axis):
    return lax.all_to_all(blocks, axis, split_axis=0, concat_axis=0, tiled=True)


def body(tokens, out_grad, expert_ids, route_weight, w_gate, w_up, w_down):
    experts = lax.axis_size("ep")
    groups = lax.axis_size("rep")
    count, quarter = tokens.shape
    ffw = w_gate.shape[2]
    main = experts * MAIN
    n, m = main // groups, experts // groups
    shape = jax.ShapeDtypeStruct
    packed = pltpu.VMEM((experts, MAIN, LANES), F32)

    weights = kernel_call(
        pack_weights_kernel,
        shape((quarter, 2 * ffw), BF),
        (w_gate[0], w_up[0]),
        0,
        vmem=60,
    )
    weights = lax.all_gather(weights, "rep", axis=0)
    ids = expert_ids.T
    sent = kernel_call(
        dispatch_kernel,
        shape((main, 2 * quarter + LANES), BF),
        (ids, route_weight.T, tokens, out_grad),
        4 * main * count * quarter,
        (
            packed,
            pltpu.VMEM((count, quarter), BF),
            pltpu.VMEM((count, quarter), BF),
            pltpu.SemaphoreType.DMA((2,)),
        ),
        in_hbm=(2, 3),
    )
    rows = exchange(sent.reshape(experts, MAIN, -1), "ep").reshape(main, -1)
    back_parts, token_rows = kernel_call(
        grad_products_kernel,
        (shape((main + experts, ffw), BF), shape((main, quarter + LANES), BF)),
        (rows, w_down[0]),
        2 * (main + experts) * quarter * ffw,
        (packed,),
    )
    token_rows, back_parts, weights = lax.optimization_barrier(
        (token_rows, back_parts, weights)
    )
    back_sums = lax.psum_scatter(back_parts, "rep", scatter_dimension=0, tiled=True)
    wide_rows = exchange(token_rows.reshape(groups, n, -1), "rep")
    terms, back = kernel_call(
        expert_kernel,
        (shape((n + m, 3 * ffw), BF), shape((groups, n, quarter + LANES), BF)),
        (wide_rows, weights, back_sums),
        8 * (n + m) * groups * quarter * ffw,
        (
            pltpu.VMEM((groups, n, quarter + LANES), BF),
            pltpu.VMEM((groups, quarter, 2 * ffw), BF),
            pltpu.VMEM((n + m, ffw), BF),
            pltpu.VMEM((m, MAIN, LANES), F32),
            pltpu.SemaphoreType.DMA((2, groups + 1)),
        ),
        in_hbm=(0, 1, 2),
        vmem=60,
    )
    terms = lax.all_gather(terms, "rep", axis=0, tiled=True)
    back = exchange(back, "rep")
    returned = exchange(back.reshape(experts, MAIN, -1), "ep").reshape(main, -1)
    grad_gate, grad_up = kernel_call(
        token_weights_kernel,
        (shape((quarter, ffw), BF), shape((quarter, ffw), BF)),
        (rows, terms),
        4 * (main + experts) * quarter * ffw,
        (packed,),
    )
    grad_down = kernel_call(
        down_weights_kernel,
        shape((ffw, quarter), BF),
        (rows, terms),
        2 * (main + experts) * quarter * ffw,
        (packed,),
    )
    ids, grad_gate, grad_up, grad_down = lax.optimization_barrier(
        (ids, grad_gate, grad_up, grad_down)
    )
    token_grad = kernel_call(
        combine_kernel,
        shape((count, quarter), BF),
        (ids, returned),
        2 * main * count * quarter,
        (packed,),
    )
    return token_grad, grad_gate[None], grad_up[None], grad_down[None]


def solution(mesh):
    rows = P("ep", "rep")
    by_width = P("ep", "rep", None)
    last = P("ep", None, "rep")
    return jax.shard_map(
        body,
        mesh=mesh,
        in_specs=(rows, rows, P("ep", None), P("ep", None), by_width, by_width, last),
        out_specs=(rows, by_width, by_width, last),
        check_vma=False,
    )
```
